256 devices in a mesh: path: 32 (over x, z), mp: 2 (over core), period: 4 (over y).
Axes of the slice: x: 4, y: 4, z: 8, core: 2. Of those that a mesh axis runs over, the one named last changes fastest.
Arguments:
- tiles: bfloat16 [4096, 256, 256], P(('path', 'mp')), may hold values from -0.375 to 0.375
- tile_rows: int32 [4096], P(('path', 'mp')), may hold values from 0 to 7
- tile_cols: int32 [4096], P(('path', 'mp')), may hold values from 0 to 1023, as said below
- tile_counts: int32 [64], P(('path', 'mp')), may hold values from 8 to 64, as said below
- data: float32 [262144], P(('period', 'path')), parts along dimension 0, may hold values from -6 to 6
Outputs:
- solution: float32 [2097152], P(('period', 'path', 'mp')), parts along dimension 0
- left_vector: float32 [262144], P(('period', 'path')), parts along dimension 0
The draws below stay inside these ranges and needn't reach their ends.
There are 4 independent parts, one for each index of `period`. The reference program is written for one: setup_inputs(seed, part) draws one part's arguments, and reference() takes and returns one part's arrays. A program takes and returns all parts, laid end to end along the dimension named above; an argument that names none is the same for every part. Nothing has to cross between parts.
Inputs may be any that keep to these rules, and one draw needn't show every extreme that they name: `tile_counts`: slots from the strip's count on are unused; some strips are full. `tile_cols`: among all 64 slots of one strip, at most 8 name cell tiles t with the same t // 32, and in every strip some value of t // 32 is named by exactly 8 slots.
All inputs are finite; a program needn't handle non-finite values.
Results may differ from the reference program's by a relative error of at most 0.0066.
Values may be sent and summed in bfloat16 or wider, within the bound.
No kernel may reach another device: no remote copies, remote signals or barrier semaphores. Data moves between devices by JAX's collectives and lax.ppermute only.
A program may use at most 64 MiB of HBM per device.

```python
import jax
import jax.numpy as jnp
from jax import lax

TILE = 256
MAXT = 64
RT_DEV = 8
CT_DEV = 32
ITERS = 2
STRIPS = 64
ROWS = 65536
NCELL = 524288
N_PATH = 32
N_MP = 2


def draw_tile_counts(key, part):
    first, second = jax.random.split(jax.random.fold_in(key, 7))
    base = jax.random.randint(first, (STRIPS,), MAXT // 8, MAXT // 2 + 1)
    order = jax.random.permutation(second, STRIPS)
    return jnp.where(order < max(1, STRIPS // 8), MAXT, base).astype(jnp.int32)


def draw_tile_cols(key, part):
    keys = jax.random.split(jax.random.fold_in(key, 11), 4)
    limit = max(2, max(MAXT // 8, (MAXT + N_PATH - 1) // N_PATH))
    hot_owner = jax.random.randint(keys[0], (STRIPS, 1), 0, N_PATH)
    offset = jax.random.randint(keys[1], (STRIPS, 1), 0, N_PATH - 1)
    slot = jnp.arange(MAXT, dtype=jnp.int32)[None, :]
    others = (hot_owner + 1 + (slot - limit + offset) % (N_PATH - 1)) % N_PATH
    owner = jnp.where(slot < limit, hot_owner, others)
    scores = jax.random.randint(keys[2], (STRIPS, MAXT), 0, 1 << 20) * MAXT + slot
    order = jnp.argsort(scores, axis=1, stable=True)
    owner = jnp.take_along_axis(owner, order, axis=1)
    inside = jax.random.randint(keys[3], (STRIPS, MAXT), 0, CT_DEV)
    return (owner * CT_DEV + inside).reshape(-1).astype(jnp.int32)


def plant(values, key, smallest, top_value):
    dims = values.shape
    spot = [jax.random.randint(jax.random.fold_in(key, axis), (), 0, dims[axis]) for axis in range(len(dims))]
    values = values.at[tuple(spot)].set(smallest)
    longest = dims.index(max(dims))
    spot[longest] = (spot[longest] + 1) % dims[longest]
    return values.at[tuple(spot)].set(top_value)


def shard_levels(stream_key, dims, cuts, low, largest):
    factor_of, own = 1.0, jax.random.fold_in(stream_key, 6)
    for dim, shards_of in cuts:
        steps = jnp.exp(jax.random.uniform(jax.random.fold_in(own, dim), (shards_of,), jnp.float32, low / len(cuts), largest / len(cuts)))
        factor_of = factor_of * jnp.repeat(steps, dims[dim] // shards_of).reshape([-1 if axis == dim else 1 for axis in range(len(dims))])
    return factor_of


def scatter_about(stream_key, extent, width, bound, pieces=(), kind=jnp.bfloat16):
    level = shard_levels(stream_key, extent, pieces, -0.22, 0.18) if pieces else 1.0
    result = jax.random.normal(stream_key, extent, jnp.float32) * width * level
    return jnp.minimum(jnp.maximum(result, -bound), bound).astype(kind)


def setup_inputs(seed: int = 0, part: int = 0) -> dict:
    arg_keys = jax.random.split(jax.random.key(seed), 6)
    own_keys = jax.random.split(jax.random.fold_in(arg_keys[5], part), 6)
    return {
        "tiles": scatter_about(arg_keys[0], (STRIPS * MAXT, TILE, TILE), TILE ** -0.5, 0.375, ((0, 64),)),
        "tile_rows": plant(jax.random.randint(arg_keys[1], (STRIPS * MAXT,), 0, RT_DEV), jax.random.fold_in(arg_keys[1], 1), 0, RT_DEV - 1).astype(jnp.int32),
        "tile_cols": draw_tile_cols(jax.random.fold_in(arg_keys[5], 71), part),
        "tile_counts": draw_tile_counts(jax.random.fold_in(arg_keys[5], 71), part),
        "data": scatter_about(own_keys[4], (ROWS,), 1.0, 6.0, ((0, 32),), jnp.float32),
    }


def reference(tiles, tile_rows, tile_cols, tile_counts, data):
    slots = lax.iota(jnp.int32, STRIPS * MAXT)
    strip = slots // MAXT
    path_index = strip // N_MP
    half_index = strip % N_MP
    live = (slots % MAXT < tile_counts[strip]).astype(jnp.float32)
    cell_tile = (tile_cols // CT_DEV * N_MP + half_index) * CT_DEV + tile_cols % CT_DEV
    row_tile = path_index * RT_DEV + tile_rows
    blocks = tiles.reshape(STRIPS, MAXT, TILE, TILE)

    def forward(vec_b):
        picked = vec_b.reshape(-1, TILE)[cell_tile].reshape(STRIPS, MAXT, TILE)
        prods = lax.map(lambda pair: jnp.einsum('sij,sj->si', pair[0].astype(jnp.float32), pair[1].astype(jnp.float32), precision=lax.Precision.HIGHEST), (blocks, picked))
        prods = prods.reshape(-1, TILE) * live[:, None]
        return jax.ops.segment_sum(prods, row_tile, num_segments=ROWS // TILE).reshape(-1)

    def backward(vec_b):
        picked = vec_b.reshape(-1, TILE)[row_tile].reshape(STRIPS, MAXT, TILE)
        prods = lax.map(lambda pair: jnp.einsum('sij,si->sj', pair[0].astype(jnp.float32), pair[1].astype(jnp.float32), precision=lax.Precision.HIGHEST), (blocks, picked))
        prods = prods.reshape(-1, TILE) * live[:, None]
        return jax.ops.segment_sum(prods, cell_tile, num_segments=NCELL // TILE).reshape(-1)
    beta = jnp.sqrt(jnp.sum(data * data) + 1e-12)
    left = data / beta
    phibar = beta
    right = backward(left.astype(jnp.bfloat16))
    alpha = jnp.sqrt(jnp.sum(right * right) + 1e-12)
    right = right / alpha
    search = right
    rhobar = alpha
    solution = jnp.zeros((NCELL,), jnp.float32)
    for step in range(ITERS):
        left = forward(right.astype(jnp.bfloat16)) - alpha * left
        beta = jnp.sqrt(jnp.sum(left * left) + 1e-12)
        left = left / beta
        right = backward(left.astype(jnp.bfloat16)) - beta * right
        alpha = jnp.sqrt(jnp.sum(right * right) + 1e-12)
        right = right / alpha
        rho = jnp.sqrt(rhobar * rhobar + beta * beta)
        cosine = rhobar / rho
        sine = beta / rho
        theta = sine * alpha
        rhobar = -cosine * alpha
        phi = cosine * phibar
        phibar = sine * phibar
        solution = solution + phi / rho * search
        search = right - theta / rho * search
    return (solution, left * jnp.sqrt(jnp.float32(ROWS)))
```

```python
import jax
import jax.numpy as jnp
from jax import lax
from jax.experimental import pallas as pl
from jax.experimental.pallas import tpu as pltpu
from jax.sharding import PartitionSpec as P

CT_DEV = 32
EPS = 1e-12
CHUNKS = 8
META = 128
F32 = jnp.float32
BF16 = jnp.bfloat16
VMEM = pl.BlockSpec(memory_space=pltpu.VMEM)
SMEM = pl.BlockSpec(memory_space=pltpu.SMEM)
ANY = pl.BlockSpec(memory_space=pl.ANY)


def iota(shape, dim):
    return lax.broadcasted_iota(jnp.int32, shape, dim)


def onehot(mask):
    return jnp.where(mask, 1.0, 0.0).astype(BF16)


def dot(a, b, ca, cb):
    return lax.dot_general(a, b, (((ca,), (cb,)), ((), ())), preferred_element_type=F32)


def total(x):
    return jnp.sum(jnp.sum(x, axis=1, keepdims=True), axis=0, keepdims=True)


def load_pairs(ref, rows):
    return jnp.concatenate(
        [ref[pl.ds(0, rows, stride=2), :], ref[pl.ds(1, rows, stride=2), :]], axis=1
    )


def store_pairs(ref, value, rows):
    half = value.shape[1] // 2
    ref[pl.ds(0, rows, stride=2), :] = value[:, :half]
    ref[pl.ds(1, rows, stride=2), :] = value[:, half:]


def pieces(lane, value):
    high = value.astype(BF16).astype(F32)
    rest = value - high
    middle = rest.astype(BF16).astype(F32)
    low = rest - middle
    return jnp.where(lane == 1, high, jnp.where(lane == 2, middle, jnp.where(lane == 3, low, 0.0)))


def sum_pieces(meta, limit):
    lane = iota(meta.shape, 1)
    return total(jnp.where((lane >= 1) & (lane <= 3), meta, 0.0)) * (1.0 / limit)


def column_of(row):
    n = row.shape[1]
    return jnp.sum(jnp.where(iota((n, n), 0) == iota((n, n), 1), row, 0), axis=1, keepdims=True)


def placement(cols_ref, count_ref, npath, limit):
    cols = cols_ref[...]
    slots = cols.shape[1]
    owner = lax.div(cols, CT_DEV)
    inside = cols - owner * CT_DEV
    owner_col = column_of(owner)
    earlier = iota((slots, slots), 0) < iota((slots, slots), 1)
    same = (owner_col == owner) & earlier
    rank = jnp.sum(jnp.where(same, 1, 0), axis=0, keepdims=True)
    live = iota(cols.shape, 1) < count_ref[0]
    target = jnp.where(live, owner * limit + rank, -1)
    place = onehot(iota((npath * limit, slots), 0) == target)
    return place, inside


def start_tiles(tiles_ref, held, sems):
    step = held.shape[0] // CHUNKS
    copies = []
    for k in range(CHUNKS):
        part = pl.ds(k * step, step)
        copies.append(pltpu.make_async_copy(tiles_ref.at[part], held.at[part], sems.at[k]))
        copies[-1].start()
    return copies


def backward(copies, held, rows_ref, left):
    slots, tile = held.shape[0], held.shape[1]
    row_tiles = left.shape[0]
    row_hot = onehot(iota((row_tiles, slots), 0) == rows_ref[...])
    picked = dot(row_hot, left.astype(BF16), 0, 0)
    step = slots // CHUNKS
    sub = iota((step, tile), 0)
    out = []
    for k in range(CHUNKS):
        copies[k].wait()
        block = picked[k * step : (k + 1) * step]
        acc = jnp.zeros((step, tile), F32)
        for i in range(step):
            acc += dot(jnp.where(sub == i, block, 0.0).astype(BF16), held[k * step + i], 1, 0)
        out.append(acc.astype(BF16))
    return jnp.concatenate(out, axis=0)


def forward(copies, held, rows_ref, picked, row_tiles):
    slots, tile = held.shape[0], held.shape[1]
    step = slots // CHUNKS
    row_hot = jnp.where(iota((row_tiles, slots), 0) == rows_ref[...], 1.0, 0.0)
    acc = jnp.zeros((row_tiles, tile), F32)
    for k in range(CHUNKS):
        copies[k].wait()
        for i in range(step):
            s = k * step + i
            lhs = row_hot[:, s : s + 1] * picked[s : s + 1, :]
            acc += dot(lhs.astype(BF16), held[s], 1, 1)
    return acc


def send_terms(send_ref, place, inside, prods, norm):
    npath, limit, width = send_ref.shape
    slots, tile = prods.shape
    meta = jnp.where(iota((slots, META), 1) == 0, column_of(inside) + 1, 0)
    out = dot(place, jnp.concatenate([prods, meta.astype(F32).astype(BF16)], axis=1), 1, 0)
    lane = iota((npath * limit, META), 1)
    tail = out[:, tile:] + pieces(lane, norm)
    full = jnp.concatenate([out[:, :tile], tail], axis=1)
    send_ref[...] = full.astype(BF16).reshape(npath, limit, width)


def first_kernel(count_ref, rows_ref, cols_ref, data_ref, tiles_ref, send_ref, held, sems):
    npath, limit, _ = send_ref.shape
    copies = start_tiles(tiles_ref, held, sems)
    place, inside = placement(cols_ref, count_ref, npath, limit)
    left = load_pairs(data_ref, data_ref.shape[0] // 2)
    prods = backward(copies, held, rows_ref, left)
    send_terms(send_ref, place, inside, prods, total(left * left))


def owner_parts(recv_ref, index_ref):
    npath, limit, width = recv_ref.shape
    rows = npath * limit
    tile = width - META
    recv = recv_ref[...].reshape(rows, width)
    index = index_ref[...].reshape(rows, width)[:, tile:].astype(F32)
    hot = onehot(index[:, 0:1].astype(jnp.int32) == iota((rows, CT_DEV), 1) + 1)
    own = dot(hot, recv[:, :tile], 0, 0)
    return hot, own, sum_pieces(recv[:, tile:].astype(F32), limit)


def answer(send_ref, hot, own, norm):
    npath, limit, width = send_ref.shape
    picked = dot(hot, own.astype(BF16), 1, 0)
    tail = pieces(iota((npath * limit, META), 1), norm)
    full = jnp.concatenate([picked, tail], axis=1)
    send_ref[...] = full.astype(BF16).reshape(npath, limit, width)


def spread(value):
    return jnp.broadcast_to(value, (1, META))


def first_owner_kernel(recv_ref, send_ref, own_ref, scal_ref):
    hot, own, norm = owner_parts(recv_ref, recv_ref)
    own_ref[...] = own
    scal_ref[...] = jnp.broadcast_to(norm, scal_ref.shape)
    answer(send_ref, hot, own, total(own * own))


def forward_kernel(count_ref, rows_ref, cols_ref, recv_ref, tiles_ref, out_ref, held, sems):
    npath, limit, width = recv_ref.shape
    tile = width - META
    copies = start_tiles(tiles_ref, held, sems)
    place, _ = placement(cols_ref, count_ref, npath, limit)
    recv = recv_ref[...].reshape(npath * limit, width)
    picked = dot(place, recv[:, :tile], 0, 0)
    norm = sum_pieces(recv[:, tile:].astype(F32), limit)
    row_tiles = out_ref.shape[0]
    acc = forward(copies, held, rows_ref, picked, row_tiles)
    out_ref[...] = jnp.concatenate([acc, jnp.broadcast_to(norm, (row_tiles, META))], axis=1)


def second_kernel(
    count_ref, rows_ref, cols_ref, data_ref, sums_ref, scal_ref, tiles_ref,
    send_ref, left_ref, out_scal_ref, held, sems,
):
    npath, limit, width = send_ref.shape
    tile = width - META
    copies = start_tiles(tiles_ref, held, sems)
    place, inside = placement(cols_ref, count_ref, npath, limit)
    beta_sq = scal_ref[0:1, 0:1] + EPS
    beta = jnp.sqrt(beta_sq)
    alpha = jnp.sqrt(sums_ref[0:1, tile : tile + 1] / beta_sq + EPS)
    data = load_pairs(data_ref, data_ref.shape[0] // 2)
    left = sums_ref[:, :tile] / (beta * alpha) - (alpha / beta) * data
    left_ref[...] = left
    out_scal_ref[...] = jnp.zeros_like(out_scal_ref)
    out_scal_ref[0:1, :] = spread(beta)
    out_scal_ref[1:2, :] = spread(alpha)
    prods = backward(copies, held, rows_ref, left)
    send_terms(send_ref, place, inside, prods, total(left * left))


def second_owner_kernel(recv_ref, index_ref, own_ref, scal_ref, send_ref, next_ref, out_scal_ref):
    hot, terms, norm = owner_parts(recv_ref, index_ref)
    beta0, alpha0 = scal_ref[0:1, 0:1], scal_ref[1:2, 0:1]
    beta1 = jnp.sqrt(norm + EPS)
    own = terms / beta1 - own_ref[...] * (beta1 / (beta0 * alpha0))
    next_ref[...] = own
    out_scal_ref[...] = jnp.broadcast_to(beta1, out_scal_ref.shape)
    answer(send_ref, hot, own, total(own * own))


def third_kernel(sums_ref, left_ref, beta_ref, send_ref, next_ref, alpha_ref):
    npath, limit, _ = send_ref.shape
    tile = left_ref.shape[1]
    alpha = jnp.sqrt(sums_ref[0:1, tile : tile + 1] + EPS)
    left = sums_ref[:, :tile] / alpha - left_ref[...] * (alpha / beta_ref[0:1, 0:1])
    next_ref[...] = left
    alpha_ref[...] = jnp.broadcast_to(alpha, alpha_ref.shape)
    tail = pieces(iota((npath * limit, META), 1), total(left * left))
    send_ref[...] = tail.astype(BF16).reshape(npath, limit, META)


def final_kernel(
    total_rows, recv_ref, left_ref, own0_ref, own1_ref, scal_ref, beta_ref, alpha_ref,
    solution_ref, out_ref,
):
    npath, limit, _ = recv_ref.shape
    norm = sum_pieces(recv_ref[...].astype(F32).reshape(npath * limit, META), limit)
    beta2 = jnp.sqrt(norm + EPS)
    beta0, alpha0 = scal_ref[0:1, 0:1], scal_ref[1:2, 0:1]
    beta1, alpha1 = beta_ref[0:1, 0:1], alpha_ref[0:1, 0:1]
    rho1 = jnp.sqrt(alpha0 * alpha0 + beta1 * beta1)
    cosine, sine = alpha0 / rho1, beta1 / rho1
    theta = sine * alpha1
    rhobar = -cosine * alpha1
    phi1, phibar = cosine * beta0, sine * beta0
    rho2 = jnp.sqrt(rhobar * rhobar + beta2 * beta2)
    phi2 = rhobar / rho2 * phibar
    right0 = own0_ref[...] / (beta0 * alpha0)
    right1 = own1_ref[...] / alpha1
    search = right1 - (theta / rho1) * right0
    answer_ = (phi1 / rho1) * right0 + (phi2 / rho2) * search
    store_pairs(solution_ref, answer_, answer_.shape[0])
    left = left_ref[...] * (total_rows**0.5 / beta2)
    store_pairs(out_ref, left, left.shape[0])


def call(kernel, ins, outs, scratch=(), flops=0, moved=0):
    shapes = [jax.ShapeDtypeStruct(s, d) for s, d in outs]
    return pl.pallas_call(
        kernel,
        in_specs=ins,
        out_specs=[VMEM] * len(outs),
        out_shape=shapes,
        scratch_shapes=scratch,
        cost_estimate=pl.CostEstimate(flops=flops, bytes_accessed=moved, transcendentals=0),
    )


def on_device(tiles, tile_rows, tile_cols, tile_counts, data):
    slots, tile, _ = tiles.shape
    row_tiles = data.shape[0] // tile
    npath = lax.axis_size("path")
    limit = max(2, max(slots // 8, (slots + npath - 1) // npath))
    width = tile + META
    rows = tile_rows.reshape(1, slots)
    cols = tile_cols.reshape(1, slots)
    data = data.reshape(row_tiles * 2, tile // 2)
    held = [pltpu.VMEM(tiles.shape, tiles.dtype), pltpu.SemaphoreType.DMA((CHUNKS,))]
    payload = ((npath, limit, width), BF16)
    scal = ((8, META), F32)
    own_shape = ((CT_DEV, tile), F32)
    left_shape = ((row_tiles, tile), F32)
    work = dict(scratch=held, flops=2 * 8 * tiles.size, moved=2 * tiles.size)

    def swap(x):
        return lax.all_to_all(x, "path", 0, 0, tiled=True)

    (send,) = call(first_kernel, [SMEM, VMEM, VMEM, VMEM, ANY], [payload], **work)(
        tile_counts, rows, cols, data, tiles
    )
    index = swap(send)
    send, own0, scal0 = call(first_owner_kernel, [VMEM], [payload, own_shape, scal])(index)
    recv = swap(send)
    pass_forward = call(
        forward_kernel, [SMEM, VMEM, VMEM, VMEM, ANY], [((row_tiles, width), F32)], **work
    )
    (part,) = pass_forward(tile_counts, rows, cols, recv, tiles)
    sums = lax.psum(part, "mp")
    send, left, scal1 = call(
        second_kernel, [SMEM] + [VMEM] * 5 + [ANY], [payload, left_shape, scal], **work
    )(tile_counts, rows, cols, data, sums, scal0, tiles)
    recv = swap(send)
    send, own1, beta1 = call(second_owner_kernel, [VMEM] * 4, [payload, own_shape, scal])(
        recv, index, own0, scal1
    )
    recv = swap(send)
    (part,) = pass_forward(tile_counts, rows, cols, recv, tiles)
    sums = lax.psum(part, "mp")
    send, left, alpha1 = call(
        third_kernel, [VMEM] * 3, [((npath, limit, META), BF16), left_shape, scal]
    )(sums, left, beta1)
    recv = swap(send)
    total_rows = row_tiles * tile * npath

    def last(*refs):
        final_kernel(total_rows, *refs)

    solution, left = call(
        last, [VMEM] * 7, [((CT_DEV * 2, tile // 2), F32), ((row_tiles * 2, tile // 2), F32)]
    )(recv, left, own0, own1, scal1, beta1, alpha1)
    return solution.reshape(-1), left.reshape(-1)


def solution(mesh):
    placed = (
        P(("path", "mp"), None, None),
        P(("path", "mp")),
        P(("path", "mp")),
        P(("path", "mp")),
        P(("period", "path")),
    )
    return jax.shard_map(
        on_device,
        mesh=mesh,
        in_specs=placed,
        out_specs=(P(("period", "path", "mp")), P(("period", "path"))),
        check_vma=False,
    )
```

```python
import jax
import jax.numpy as jnp
from jax import lax
from jax.experimental import pallas as pl
from jax.experimental.pallas import tpu as pltpu
from jax.sharding import PartitionSpec as P

CT_DEV = 32
EPS = 1e-12
CHUNKS = 8
META = 128
LIMIT = 12 << 20
FIRST_LIMIT = 50 << 20
F32 = jnp.float32
BF16 = jnp.bfloat16
VMEM = pl.BlockSpec(memory_space=pltpu.VMEM)
SMEM = pl.BlockSpec(memory_space=pltpu.SMEM)
HBM = pl.BlockSpec(memory_space=pltpu.HBM)


def iota(shape, dim):
    return lax.broadcasted_iota(jnp.int32, shape, dim)


def onehot(mask):
    return jnp.where(mask, 1.0, 0.0).astype(BF16)


def dot(a, b, ca, cb):
    return lax.dot_general(a, b, (((ca,), (cb,)), ((), ())), preferred_element_type=F32)


def total(x):
    return jnp.sum(jnp.sum(x, axis=1, keepdims=True), axis=0, keepdims=True)


def load_pairs(ref, rows):
    return jnp.concatenate(
        [ref[pl.ds(0, rows, stride=2), :], ref[pl.ds(1, rows, stride=2), :]], axis=1
    )


def store_pairs(ref, value, rows):
    half = value.shape[1] // 2
    ref[pl.ds(0, rows, stride=2), :] = value[:, :half]
    ref[pl.ds(1, rows, stride=2), :] = value[:, half:]


def pieces(lane, value):
    high = value.astype(BF16).astype(F32)
    rest = value - high
    middle = rest.astype(BF16).astype(F32)
    low = rest - middle
    return jnp.where(lane == 1, high, jnp.where(lane == 2, middle, jnp.where(lane == 3, low, 0.0)))


def sum_pieces(meta, limit):
    lane = iota(meta.shape, 1)
    return total(jnp.where((lane >= 1) & (lane <= 3), meta, 0.0)) * (1.0 / limit)


def column_of(row):
    n = row.shape[1]
    return jnp.sum(jnp.where(iota((n, n), 0) == iota((n, n), 1), row, 0), axis=1, keepdims=True)


def placement(cols_ref, count_ref, npath, limit):
    cols = cols_ref[...]
    slots = cols.shape[1]
    owner = lax.div(cols, CT_DEV)
    inside = cols - owner * CT_DEV
    owner_col = column_of(owner)
    earlier = iota((slots, slots), 0) < iota((slots, slots), 1)
    same = (owner_col == owner) & earlier
    rank = jnp.sum(jnp.where(same, 1, 0), axis=0, keepdims=True)
    live = iota(cols.shape, 1) < count_ref[0]
    target = jnp.where(live, owner * limit + rank, -1)
    place = onehot(iota((npath * limit, slots), 0) == target)
    return place, inside


def start_tiles(tiles_ref, held, sems):
    step = held.shape[0] // CHUNKS
    copies = []
    for k in range(CHUNKS):
        part = pl.ds(k * step, step)
        copies.append(pltpu.make_async_copy(tiles_ref.at[part], held.at[part], sems.at[k]))
        copies[-1].start()
    return copies


def backward(held, rows_ref, left, copies=None):
    slots, tile = held.shape[0], held.shape[1]
    row_tiles = left.shape[0]
    row_hot = onehot(iota((row_tiles, slots), 0) == rows_ref[...])
    picked = dot(row_hot, left.astype(BF16), 0, 0)
    step = slots // CHUNKS
    sub = iota((step, tile), 0)
    out = []
    for k in range(CHUNKS):
        if copies is not None:
            copies[k].wait()
        block = picked[k * step : (k + 1) * step]
        acc = jnp.zeros((step, tile), F32)
        for i in range(step):
            acc += dot(jnp.where(sub == i, block, 0.0).astype(BF16), held[k * step + i], 1, 0)
        out.append(acc.astype(BF16))
    return jnp.concatenate(out, axis=0)


def forward(held, rows_ref, picked, row_tiles):
    slots, tile = held.shape[0], held.shape[1]
    step = slots // CHUNKS
    row_hot = jnp.where(iota((row_tiles, slots), 0) == rows_ref[...], 1.0, 0.0)
    acc = jnp.zeros((row_tiles, tile), F32)
    for k in range(CHUNKS):
        for i in range(step):
            s = k * step + i
            lhs = row_hot[:, s : s + 1] * picked[s : s + 1, :]
            acc += dot(lhs.astype(BF16), held[s], 1, 1)
    return acc


def send_terms(send_ref, place, inside, prods, norm):
    npath, limit, width = send_ref.shape
    slots, tile = prods.shape
    meta = jnp.where(iota((slots, META), 1) == 0, column_of(inside) + 1, 0)
    out = dot(place, jnp.concatenate([prods, meta.astype(F32).astype(BF16)], axis=1), 1, 0)
    lane = iota((npath * limit, META), 1)
    tail = out[:, tile:] + pieces(lane, norm)
    full = jnp.concatenate([out[:, :tile], tail], axis=1)
    send_ref[...] = full.astype(BF16).reshape(npath, limit, width)


def first_kernel(count_ref, rows_ref, cols_ref, data_ref, tiles_ref, send_ref, held_ref, sems):
    npath, limit, _ = send_ref.shape
    copies = start_tiles(tiles_ref, held_ref, sems)
    place, inside = placement(cols_ref, count_ref, npath, limit)
    left = load_pairs(data_ref, data_ref.shape[0] // 2)
    prods = backward(held_ref, rows_ref, left, copies)
    send_terms(send_ref, place, inside, prods, total(left * left))


def owner_parts(recv_ref, index_ref):
    npath, limit, width = recv_ref.shape
    rows = npath * limit
    tile = width - META
    recv = recv_ref[...].reshape(rows, width)
    index = index_ref[...].reshape(rows, width)[:, tile:].astype(F32)
    hot = onehot(index[:, 0:1].astype(jnp.int32) == iota((rows, CT_DEV), 1) + 1)
    own = dot(hot, recv[:, :tile], 0, 0)
    return hot, own, sum_pieces(recv[:, tile:].astype(F32), limit)


def answer(send_ref, hot, own, norm):
    npath, limit, width = send_ref.shape
    picked = dot(hot, own.astype(BF16), 1, 0)
    tail = pieces(iota((npath * limit, META), 1), norm)
    full = jnp.concatenate([picked, tail], axis=1)
    send_ref[...] = full.astype(BF16).reshape(npath, limit, width)


def spread(value):
    return jnp.broadcast_to(value, (1, META))


def first_owner_kernel(recv_ref, send_ref, own_ref, scal_ref):
    hot, own, norm = owner_parts(recv_ref, recv_ref)
    own_ref[...] = own
    scal_ref[...] = jnp.broadcast_to(norm, scal_ref.shape)
    answer(send_ref, hot, own, total(own * own))


def forward_kernel(count_ref, rows_ref, cols_ref, recv_ref, tiles_ref, out_ref):
    npath, limit, width = recv_ref.shape
    tile = width - META
    place, _ = placement(cols_ref, count_ref, npath, limit)
    recv = recv_ref[...].reshape(npath * limit, width)
    picked = dot(place, recv[:, :tile], 0, 0)
    norm = sum_pieces(recv[:, tile:].astype(F32), limit)
    row_tiles = out_ref.shape[0]
    acc = forward(tiles_ref, rows_ref, picked, row_tiles)
    out_ref[...] = jnp.concatenate([acc, jnp.broadcast_to(norm, (row_tiles, META))], axis=1)


def second_kernel(
    count_ref, rows_ref, cols_ref, data_ref, part_ref, other_ref, scal_ref, tiles_ref,
    send_ref, left_ref, out_scal_ref,
):
    npath, limit, width = send_ref.shape
    tile = width - META
    place, inside = placement(cols_ref, count_ref, npath, limit)
    sums = part_ref[...] + other_ref[...]
    beta_sq = scal_ref[0:1, 0:1] + EPS
    beta = jnp.sqrt(beta_sq)
    alpha = jnp.sqrt(sums[0:1, tile : tile + 1] / beta_sq + EPS)
    data = load_pairs(data_ref, data_ref.shape[0] // 2)
    left = sums[:, :tile] / (beta * alpha) - (alpha / beta) * data
    left_ref[...] = left
    out_scal_ref[...] = jnp.zeros_like(out_scal_ref)
    out_scal_ref[0:1, :] = spread(beta)
    out_scal_ref[1:2, :] = spread(alpha)
    prods = backward(tiles_ref, rows_ref, left)
    send_terms(send_ref, place, inside, prods, total(left * left))


def second_owner_kernel(recv_ref, index_ref, own_ref, scal_ref, send_ref, next_ref, out_scal_ref):
    hot, terms, norm = owner_parts(recv_ref, index_ref)
    beta0, alpha0 = scal_ref[0:1, 0:1], scal_ref[1:2, 0:1]
    beta1 = jnp.sqrt(norm + EPS)
    own = terms / beta1 - own_ref[...] * (beta1 / (beta0 * alpha0))
    next_ref[...] = own
    out_scal_ref[...] = jnp.broadcast_to(beta1, out_scal_ref.shape)
    answer(send_ref, hot, own, total(own * own))


def third_kernel(part_ref, other_ref, left_ref, beta_ref, send_ref, next_ref, alpha_ref):
    npath, limit, _ = send_ref.shape
    tile = left_ref.shape[1]
    sums = part_ref[...] + other_ref[...]
    alpha = jnp.sqrt(sums[0:1, tile : tile + 1] + EPS)
    left = sums[:, :tile] / alpha - left_ref[...] * (alpha / beta_ref[0:1, 0:1])
    next_ref[...] = left
    alpha_ref[...] = jnp.broadcast_to(alpha, alpha_ref.shape)
    tail = pieces(iota((npath * limit, META), 1), total(left * left))
    send_ref[...] = tail.astype(BF16).reshape(npath, limit, META)


def final_kernel(
    total_rows, recv_ref, left_ref, own0_ref, own1_ref, scal_ref, beta_ref, alpha_ref,
    solution_ref, out_ref,
):
    npath, limit, _ = recv_ref.shape
    norm = sum_pieces(recv_ref[...].astype(F32).reshape(npath * limit, META), limit)
    beta2 = jnp.sqrt(norm + EPS)
    beta0, alpha0 = scal_ref[0:1, 0:1], scal_ref[1:2, 0:1]
    beta1, alpha1 = beta_ref[0:1, 0:1], alpha_ref[0:1, 0:1]
    rho1 = jnp.sqrt(alpha0 * alpha0 + beta1 * beta1)
    cosine, sine = alpha0 / rho1, beta1 / rho1
    theta = sine * alpha1
    rhobar = -cosine * alpha1
    phi1, phibar = cosine * beta0, sine * beta0
    rho2 = jnp.sqrt(rhobar * rhobar + beta2 * beta2)
    phi2 = rhobar / rho2 * phibar
    right0 = own0_ref[...] / (beta0 * alpha0)
    right1 = own1_ref[...] / alpha1
    search = right1 - (theta / rho1) * right0
    answer_ = (phi1 / rho1) * right0 + (phi2 / rho2) * search
    store_pairs(solution_ref, answer_, answer_.shape[0])
    left = left_ref[...] * (total_rows**0.5 / beta2)
    store_pairs(out_ref, left, left.shape[0])


def call(kernel, ins, outs, scratch=(), flops=0, moved=0, room=LIMIT):
    shapes = [jax.ShapeDtypeStruct(s, d) for s, d in outs]
    return pl.pallas_call(
        kernel,
        in_specs=ins,
        out_specs=[VMEM] * len(outs),
        out_shape=shapes,
        scratch_shapes=scratch,
        compiler_params=pltpu.CompilerParams(vmem_limit_bytes=room),
        cost_estimate=pl.CostEstimate(flops=flops, bytes_accessed=moved, transcendentals=0),
    )


def on_device(tiles, tile_rows, tile_cols, tile_counts, data):
    slots, tile, _ = tiles.shape
    row_tiles = data.shape[0] // tile
    npath = lax.axis_size("path")
    limit = max(2, max(slots // 8, (slots + npath - 1) // npath))
    width = tile + META
    rows = tile_rows.reshape(1, slots)
    cols = tile_cols.reshape(1, slots)
    data = data.reshape(row_tiles * 2, tile // 2)
    payload = ((npath, limit, width), BF16)
    scal = ((8, META), F32)
    own_shape = ((CT_DEV, tile), F32)
    left_shape = ((row_tiles, tile), F32)
    work = dict(flops=2 * 8 * tiles.size, moved=2 * tiles.size)

    def swap(x):
        return lax.all_to_all(x, "path", 0, 0, tiled=True)

    held = [pltpu.VMEM(tiles.shape, tiles.dtype), pltpu.SemaphoreType.DMA((CHUNKS,))]
    (send,) = call(
        first_kernel,
        [SMEM, VMEM, VMEM, VMEM, HBM],
        [payload],
        scratch=held,
        room=FIRST_LIMIT,
        **work,
    )(tile_counts, rows, cols, data, tiles)
    index = swap(send)
    send, own0, scal0 = call(first_owner_kernel, [VMEM], [payload, own_shape, scal])(index)
    recv = swap(send)
    pass_forward = call(
        forward_kernel, [SMEM, VMEM, VMEM, VMEM, VMEM], [((row_tiles, width), F32)], **work
    )
    (part,) = pass_forward(tile_counts, rows, cols, recv, tiles)
    sums = (part, lax.ppermute(part, "mp", [(0, 1), (1, 0)]))
    send, left, scal1 = call(
        second_kernel, [SMEM] + [VMEM] * 7, [payload, left_shape, scal], **work
    )(tile_counts, rows, cols, data, *sums, scal0, tiles)
    recv = swap(send)
    send, own1, beta1 = call(second_owner_kernel, [VMEM] * 4, [payload, own_shape, scal])(
        recv, index, own0, scal1
    )
    recv = swap(send)
    (part,) = pass_forward(tile_counts, rows, cols, recv, tiles)
    sums = (part, lax.ppermute(part, "mp", [(0, 1), (1, 0)]))
    send, left, alpha1 = call(
        third_kernel, [VMEM] * 4, [((npath, limit, META), BF16), left_shape, scal]
    )(*sums, left, beta1)
    recv = swap(send)
    total_rows = row_tiles * tile * npath

    def last(*refs):
        final_kernel(total_rows, *refs)

    solution, left = call(
        last, [VMEM] * 7, [((CT_DEV * 2, tile // 2), F32), ((row_tiles * 2, tile // 2), F32)]
    )(recv, left, own0, own1, scal1, beta1, alpha1)
    return solution.reshape(-1), left.reshape(-1)


def solution(mesh):
    placed = (
        P(("path", "mp"), None, None),
        P(("path", "mp")),
        P(("path", "mp")),
        P(("path", "mp")),
        P(("period", "path")),
    )
    return jax.shard_map(
        on_device,
        mesh=mesh,
        in_specs=placed,
        out_specs=(P(("period", "path", "mp")), P(("period", "path"))),
        check_vma=False,
    )
```

```python
import jax
import jax.numpy as jnp
from jax import lax
from jax.experimental import pallas as pl
from jax.experimental.pallas import tpu as pltpu
from jax.sharding import PartitionSpec as P

CT_DEV = 32
EPS = 1e-12
CHUNKS = 8
META = 128
LIMIT = 12 << 20
FIRST_LIMIT = 50 << 20
F32 = jnp.float32
BF16 = jnp.bfloat16
VMEM = pl.BlockSpec(memory_space=pltpu.VMEM)
SMEM = pl.BlockSpec(memory_space=pltpu.SMEM)
HBM = pl.BlockSpec(memory_space=pltpu.HBM)


def iota(shape, dim):
    return lax.broadcasted_iota(jnp.int32, shape, dim)


def onehot(mask):
    return jnp.where(mask, 1.0, 0.0).astype(BF16)


def dot(a, b, ca, cb):
    return lax.dot_general(a, b, (((ca,), (cb,)), ((), ())), preferred_element_type=F32)


def total(x):
    return jnp.sum(jnp.sum(x, axis=1, keepdims=True), axis=0, keepdims=True)


def load_pairs(ref, rows):
    return jnp.concatenate(
        [ref[pl.ds(0, rows, stride=2), :], ref[pl.ds(1, rows, stride=2), :]], axis=1
    )


def store_pairs(ref, value, rows):
    half = value.shape[1] // 2
    ref[pl.ds(0, rows, stride=2), :] = value[:, :half]
    ref[pl.ds(1, rows, stride=2), :] = value[:, half:]


def pieces(lane, value):
    high = value.astype(BF16).astype(F32)
    rest = value - high
    middle = rest.astype(BF16).astype(F32)
    low = rest - middle
    return jnp.where(lane == 1, high, jnp.where(lane == 2, middle, jnp.where(lane == 3, low, 0.0)))


def sum_pieces(meta):
    lane = iota(meta.shape, 1)
    return total(jnp.where((lane >= 1) & (lane <= 3), meta, 0.0))


def split(x):
    high = x.astype(BF16)
    low = (x - high.astype(F32)).astype(BF16)
    return jnp.concatenate([high, low], axis=0)


def fold(x):
    half = x.shape[0] // 2
    return x[:half] + x[half:]


def start_tiles(tiles_ref, held, sems):
    step = held.shape[0] // CHUNKS
    copies = []
    for k in range(CHUNKS):
        part = pl.ds(k * step, step)
        copies.append(pltpu.make_async_copy(tiles_ref.at[part], held.at[part], sems.at[k]))
        copies[-1].start()
    return copies


def backward(held, rows_ref, left, copies=None):
    slots, tile = held.shape[0], held.shape[1]
    row_tiles = left.shape[0]
    row_hot = onehot(iota((row_tiles, slots), 0) == rows_ref[...])
    both = split(left)
    high = dot(row_hot, both[:row_tiles], 0, 0)
    low = dot(row_hot, both[row_tiles:], 0, 0)
    step = slots // CHUNKS
    sub = iota((2 * step, tile), 0)
    out = []
    for k in range(CHUNKS):
        if copies is not None:
            copies[k].wait()
        part = slice(k * step, (k + 1) * step)
        block = jnp.concatenate([high[part], low[part]], axis=0)
        acc = jnp.zeros((2 * step, tile), F32)
        for i in range(step):
            mine = (sub == i) | (sub == i + step)
            acc += dot(jnp.where(mine, block, 0.0).astype(BF16), held[k * step + i], 1, 0)
        out.append(fold(acc).astype(BF16))
    return jnp.concatenate(out, axis=0)


def forward(held, rows_ref, picked, row_tiles):
    slots, tile = held.shape[0], held.shape[1]
    row_hot = jnp.where(iota((row_tiles, slots), 0) == rows_ref[...], 1.0, 0.0)
    acc = jnp.zeros((2 * row_tiles, tile), F32)
    for s in range(slots):
        lhs = split(row_hot[:, s : s + 1] * picked[s : s + 1, :])
        acc += dot(lhs, held[s], 1, 1)
    return fold(acc)


def cell_of(cols_ref, count_ref):
    cols = cols_ref[...]
    owner = lax.div(cols, CT_DEV)
    live = iota(cols.shape, 1) < count_ref[0]
    return jnp.where(live, owner + 1, 0), cols - owner * CT_DEV


def send_terms(send_ref, cols_ref, count_ref, prods, norm):
    npath = send_ref.shape[0]
    half = prods.shape[1] // 2
    owner, inside = cell_of(cols_ref, count_ref)
    index = jnp.concatenate([owner, inside], axis=1).astype(F32)
    sub, lane = iota((8, META), 0), iota((8, META), 1)
    meta = jnp.where(sub == 0, index, jnp.where(sub == 1, pieces(lane, norm), 0.0))
    message = jnp.concatenate([prods[:, :half], prods[:, half:], meta.astype(BF16)], axis=0)
    for q in range(npath):
        send_ref[q] = message


def first_kernel(count_ref, rows_ref, cols_ref, data_ref, tiles_ref, send_ref, held_ref, sems):
    copies = start_tiles(tiles_ref, held_ref, sems)
    left = load_pairs(data_ref, data_ref.shape[0] // 2)
    prods = backward(held_ref, rows_ref, left, copies)
    send_terms(send_ref, cols_ref, count_ref, prods, total(left * left))


def all_cells(recv_ref, index_ref, slots, full_ref):
    npath = recv_ref.shape[0]
    group = full_ref.shape[1] // slots
    acc = None
    norm = jnp.zeros((1, 1), F32)
    for b in range(npath // group):
        sources = range(b * group, (b + 1) * group)
        metas = [index_ref[q, 2 * slots :, :].astype(F32) for q in sources]
        norms = [recv_ref[q, 2 * slots :, :].astype(F32)[1:2] for q in sources]
        for n in norms:
            norm += sum_pieces(n)
        owner = jnp.concatenate([m[0:1, :slots] for m in metas], axis=1)
        inside = jnp.concatenate([m[0:1, slots:] for m in metas], axis=1)
        shape = (CT_DEV, group * slots)
        hot = jnp.where(iota(shape, 0).astype(F32) == inside, 1.0, 0.0)
        owner = jnp.broadcast_to(owner, shape)
        mask = jnp.concatenate(
            [jnp.where(owner == o + 1.0, hot, 0.0).astype(BF16) for o in range(npath)], axis=0
        )
        block = jnp.concatenate(
            [
                jnp.concatenate([recv_ref[q, :slots, :] for q in sources], axis=0),
                jnp.concatenate([recv_ref[q, slots : 2 * slots, :] for q in sources], axis=0),
            ],
            axis=1,
        )
        term = dot(mask, block, 1, 0)
        if b == 0:
            full_ref[...] = term
        else:
            full_ref[...] += term
    return norm


def pick(cols_ref, count_ref, full_ref):
    slots = cols_ref.shape[1]
    cells = full_ref.shape[0]
    live = iota((1, slots), 1) < count_ref[0]
    cell = jnp.where(live, cols_ref[...], -1)
    hot = onehot(iota((cells, slots), 0) == cell)
    full = full_ref[...]
    high = full.astype(BF16)
    low = (full - high.astype(F32)).astype(BF16)
    return dot(hot, high, 0, 0) + dot(hot, low, 0, 0)


def finish_forward(count_ref, rows_ref, cols_ref, full_ref, tiles_ref, part_ref, own_ref):
    row_tiles = part_ref.shape[0]
    full = full_ref[...]
    norm = total(full * full)
    acc = forward(tiles_ref, rows_ref, pick(cols_ref, count_ref, full_ref), row_tiles)
    part_ref[...] = jnp.concatenate([acc, jnp.broadcast_to(norm, (row_tiles, META))], axis=1)
    me = lax.axis_index("path")
    own_ref[...] = full_ref[pl.ds(pl.multiple_of(me * CT_DEV, CT_DEV), CT_DEV), :]


def spread(value):
    return jnp.broadcast_to(value, (1, META))


def first_forward_kernel(
    count_ref, rows_ref, cols_ref, recv_ref, tiles_ref, part_ref, full_ref, own_ref, scal_ref
):
    norm = all_cells(recv_ref, recv_ref, tiles_ref.shape[0], full_ref)
    scal_ref[...] = jnp.broadcast_to(norm, scal_ref.shape)
    finish_forward(count_ref, rows_ref, cols_ref, full_ref, tiles_ref, part_ref, own_ref)


def second_kernel(
    count_ref, rows_ref, cols_ref, data_ref, part_ref, other_ref, scal_ref, tiles_ref,
    send_ref, left_ref, out_scal_ref,
):
    tile = left_ref.shape[1]
    sums = part_ref[...] + other_ref[...]
    beta_sq = scal_ref[0:1, 0:1] + EPS
    beta = jnp.sqrt(beta_sq)
    alpha = jnp.sqrt(sums[0:1, tile : tile + 1] / beta_sq + EPS)
    data = load_pairs(data_ref, data_ref.shape[0] // 2)
    left = sums[:, :tile] / (beta * alpha) - (alpha / beta) * data
    left_ref[...] = left
    out_scal_ref[...] = jnp.zeros_like(out_scal_ref)
    out_scal_ref[0:1, :] = spread(beta)
    out_scal_ref[1:2, :] = spread(alpha)
    prods = backward(tiles_ref, rows_ref, left)
    send_terms(send_ref, cols_ref, count_ref, prods, total(left * left))


def second_forward_kernel(
    count_ref, rows_ref, cols_ref, recv_ref, before_ref, scal_ref, tiles_ref,
    part_ref, own_ref, out_scal_ref, full_ref,
):
    norm = all_cells(recv_ref, recv_ref, tiles_ref.shape[0], full_ref)
    beta0, alpha0 = scal_ref[0:1, 0:1], scal_ref[1:2, 0:1]
    beta1 = jnp.sqrt(norm + EPS)
    full_ref[...] = full_ref[...] / beta1 - before_ref[...] * (beta1 / (beta0 * alpha0))
    out_scal_ref[...] = jnp.broadcast_to(beta1, out_scal_ref.shape)
    finish_forward(count_ref, rows_ref, cols_ref, full_ref, tiles_ref, part_ref, own_ref)


def third_kernel(part_ref, other_ref, left_ref, beta_ref, send_ref, next_ref, alpha_ref):
    npath = send_ref.shape[0]
    tile = left_ref.shape[1]
    sums = part_ref[...] + other_ref[...]
    alpha = jnp.sqrt(sums[0:1, tile : tile + 1] + EPS)
    left = sums[:, :tile] / alpha - left_ref[...] * (alpha / beta_ref[0:1, 0:1])
    next_ref[...] = left
    alpha_ref[...] = jnp.broadcast_to(alpha, alpha_ref.shape)
    sub, lane = iota((8, META), 0), iota((8, META), 1)
    message = jnp.where(sub == 0, pieces(lane, total(left * left)), 0.0).astype(BF16)
    for q in range(npath):
        send_ref[q] = message


def final_kernel(
    total_rows, recv_ref, left_ref, own0_ref, own1_ref, scal_ref, beta_ref, alpha_ref,
    solution_ref, out_ref,
):
    npath = recv_ref.shape[0]
    norm = sum_pieces(recv_ref[...].astype(F32).reshape(npath * 8, META))
    beta2 = jnp.sqrt(norm + EPS)
    beta0, alpha0 = scal_ref[0:1, 0:1], scal_ref[1:2, 0:1]
    beta1, alpha1 = beta_ref[0:1, 0:1], alpha_ref[0:1, 0:1]
    rho1 = jnp.sqrt(alpha0 * alpha0 + beta1 * beta1)
    cosine, sine = alpha0 / rho1, beta1 / rho1
    theta = sine * alpha1
    rhobar = -cosine * alpha1
    phi1, phibar = cosine * beta0, sine * beta0
    rho2 = jnp.sqrt(rhobar * rhobar + beta2 * beta2)
    phi2 = rhobar / rho2 * phibar
    right0 = own0_ref[...] / (beta0 * alpha0)
    right1 = own1_ref[...] / alpha1
    search = right1 - (theta / rho1) * right0
    answer_ = (phi1 / rho1) * right0 + (phi2 / rho2) * search
    store_pairs(solution_ref, answer_, answer_.shape[0])
    left = left_ref[...] * (total_rows**0.5 / beta2)
    store_pairs(out_ref, left, left.shape[0])


def call(kernel, ins, outs, scratch=(), flops=0, moved=0, room=LIMIT):
    shapes = [jax.ShapeDtypeStruct(s, d) for s, d in outs]
    return pl.pallas_call(
        kernel,
        in_specs=ins,
        out_specs=[VMEM] * len(outs),
        out_shape=shapes,
        scratch_shapes=scratch,
        compiler_params=pltpu.CompilerParams(vmem_limit_bytes=room),
        cost_estimate=pl.CostEstimate(flops=flops, bytes_accessed=moved, transcendentals=0),
    )


def on_device(tiles, tile_rows, tile_cols, tile_counts, data):
    slots, tile, _ = tiles.shape
    row_tiles = data.shape[0] // tile
    npath = lax.axis_size("path")
    rows = tile_rows.reshape(1, slots)
    cols = tile_cols.reshape(1, slots)
    data = data.reshape(row_tiles * 2, tile // 2)
    held = [pltpu.VMEM(tiles.shape, tiles.dtype), pltpu.SemaphoreType.DMA((CHUNKS,))]
    payload = ((npath, 2 * slots + 8, META), BF16)
    short = ((npath, 8, META), BF16)
    scal = ((8, META), F32)
    full_shape = (npath * CT_DEV, tile)
    own_shape = ((CT_DEV, tile), F32)
    left_shape = ((row_tiles, tile), F32)
    part_shape = ((row_tiles, tile + META), F32)
    work = dict(flops=2 * 8 * tiles.size, moved=2 * tiles.size)

    def swap(x):
        return lax.all_to_all(x, "path", 0, 0, tiled=True)

    def other_half(x):
        return lax.ppermute(x, "mp", [(0, 1), (1, 0)])

    (send,) = call(
        first_kernel,
        [SMEM, VMEM, VMEM, VMEM, HBM],
        [payload],
        scratch=held,
        room=FIRST_LIMIT,
        **work,
    )(tile_counts, rows, cols, data, tiles)
    recv = swap(send)
    part, full, own0, scal0 = call(
        first_forward_kernel,
        [SMEM] + [VMEM] * 4,
        [part_shape, (full_shape, F32), own_shape, scal],
        **work,
    )(tile_counts, rows, cols, recv, tiles)
    send, left, scal1 = call(
        second_kernel, [SMEM] + [VMEM] * 7, [payload, left_shape, scal], **work
    )(tile_counts, rows, cols, data, part, other_half(part), scal0, tiles)
    recv = swap(send)
    part, own1, beta1 = call(
        second_forward_kernel,
        [SMEM] + [VMEM] * 6,
        [part_shape, own_shape, scal],
        scratch=[pltpu.VMEM(full_shape, F32)],
        **work,
    )(tile_counts, rows, cols, recv, full, scal1, tiles)
    send, left, alpha1 = call(third_kernel, [VMEM] * 4, [short, left_shape, scal])(
        part, other_half(part), left, beta1
    )
    recv = swap(send)
    total_rows = row_tiles * tile * npath

    def last(*refs):
        final_kernel(total_rows, *refs)

    solution, left = call(
        last, [VMEM] * 7, [((CT_DEV * 2, tile // 2), F32), ((row_tiles * 2, tile // 2), F32)]
    )(recv, left, own0, own1, scal1, beta1, alpha1)
    return solution.reshape(-1), left.reshape(-1)


def solution(mesh):
    placed = (
        P(("path", "mp"), None, None),
        P(("path", "mp")),
        P(("path", "mp")),
        P(("path", "mp")),
        P(("period", "path")),
    )
    return jax.shard_map(
        on_device,
        mesh=mesh,
        in_specs=placed,
        out_specs=(P(("period", "path", "mp")), P(("period", "path"))),
        check_vma=False,
    )
```

```python
import jax
import jax.numpy as jnp
from jax import lax
from jax.experimental import pallas as pl
from jax.experimental.pallas import tpu as pltpu
from jax.sharding import PartitionSpec as P

CT_DEV = 32
EPS = 1e-12
CHUNKS = 8
META = 128
LIMIT = 12 << 20
FIRST_LIMIT = 40 << 20
F32 = jnp.float32
BF16 = jnp.bfloat16
VMEM = pl.BlockSpec(memory_space=pltpu.VMEM)
HBM = pl.BlockSpec(memory_space=pltpu.HBM)


def iota(shape, dim):
    return lax.broadcasted_iota(jnp.int32, shape, dim)


def onehot(mask):
    return jnp.where(mask, 1.0, 0.0).astype(BF16)


def dot(a, b, ca, cb):
    return lax.dot_general(a, b, (((ca,), (cb,)), ((), ())), preferred_element_type=F32)


def total(x):
    return jnp.sum(jnp.sum(x, axis=1, keepdims=True), axis=0, keepdims=True)


def load_pairs(ref, rows):
    return jnp.concatenate(
        [ref[pl.ds(0, rows, stride=2), :], ref[pl.ds(1, rows, stride=2), :]], axis=1
    )


def store_pairs(ref, value, rows):
    half = value.shape[1] // 2
    ref[pl.ds(0, rows, stride=2), :] = value[:, :half]
    ref[pl.ds(1, rows, stride=2), :] = value[:, half:]


def pieces(lane, value):
    high = value.astype(BF16).astype(F32)
    rest = value - high
    middle = rest.astype(BF16).astype(F32)
    low = rest - middle
    return jnp.where(lane == 1, high, jnp.where(lane == 2, middle, jnp.where(lane == 3, low, 0.0)))


def sum_pieces(meta):
    lane = iota(meta.shape, 1)
    return total(jnp.where((lane >= 1) & (lane <= 3), meta, 0.0))


def split(x):
    high = x.astype(BF16)
    low = (x - high.astype(F32)).astype(BF16)
    return jnp.concatenate([high, low], axis=0)


def fold(x):
    half = x.shape[0] // 2
    return x[:half] + x[half:]


def data_of(table_ref):
    return load_pairs(table_ref.at[: table_ref.shape[0] - 8], (table_ref.shape[0] - 8) // 2)


def slots_of(table_ref):
    base = table_ref.shape[0] - 8
    slots = META // 2
    both = table_ref[base : base + 1, :].astype(jnp.int32)
    count = table_ref[base + 1 : base + 2, 0:1].astype(jnp.int32)
    return both[:, slots:], both[:, :slots], count


def column_of(row):
    n = row.shape[1]
    return jnp.sum(jnp.where(iota((n, n), 0) == iota((n, n), 1), row, 0), axis=1, keepdims=True)


def placement(cols, count, npath, limit):
    slots = cols.shape[1]
    owner = lax.div(cols, CT_DEV)
    inside = cols - owner * CT_DEV
    owner_col = column_of(owner)
    earlier = iota((slots, slots), 0) < iota((slots, slots), 1)
    same = (owner_col == owner) & earlier
    rank = jnp.sum(jnp.where(same, 1, 0), axis=0, keepdims=True)
    live = iota(cols.shape, 1) < count
    target = jnp.where(live, owner * limit + rank, -1)
    key = jnp.where(live, cols, -CT_DEV)
    place = onehot(iota((npath * limit, slots), 0) == target)
    return place, inside, key


def start_tiles(tiles_ref, held, sems):
    step = held.shape[0] // CHUNKS
    copies = []
    for k in range(CHUNKS):
        part = pl.ds(k * step, step)
        copies.append(pltpu.make_async_copy(tiles_ref.at[part], held.at[part], sems.at[k]))
        copies[-1].start()
    return copies


def backward(held, rows, left, copies=None):
    slots, tile = held.shape[0], held.shape[1]
    row_tiles = left.shape[0]
    row_hot = onehot(iota((row_tiles, slots), 0) == rows)
    both = split(left)
    high = dot(row_hot, both[:row_tiles], 0, 0)
    low = dot(row_hot, both[row_tiles:], 0, 0)
    step = slots // CHUNKS
    sub = iota((2 * step, tile), 0)
    out = []
    for k in range(CHUNKS):
        if copies is not None:
            copies[k].wait()
        part = slice(k * step, (k + 1) * step)
        block = jnp.concatenate([high[part], low[part]], axis=0)
        acc = jnp.zeros((2 * step, tile), F32)
        for i in range(step):
            mine = (sub == i) | (sub == i + step)
            acc += dot(jnp.where(mine, block, 0.0).astype(BF16), held[k * step + i], 1, 0)
        out.append(fold(acc).astype(BF16))
    return jnp.concatenate(out, axis=0)


def forward(held, rows, picked, row_tiles, exact):
    slots, tile = held.shape[0], held.shape[1]
    row_hot = jnp.where(iota((row_tiles, slots), 0) == rows, 1.0, 0.0)
    acc = jnp.zeros((row_tiles if exact else 2 * row_tiles, tile), F32)
    for s in range(slots):
        lhs = row_hot[:, s : s + 1] * picked[s : s + 1, :]
        acc += dot(lhs.astype(BF16) if exact else split(lhs), held[s], 1, 1)
    return acc if exact else fold(acc)


def first_kernel(table_ref, tiles_ref, send_ref, held_ref, sems):
    npath, limit, width = send_ref.shape
    copies = start_tiles(tiles_ref, held_ref, sems)
    left = data_of(table_ref)
    rows, cols, count = slots_of(table_ref)
    place, inside, key = placement(cols, count, npath, limit)
    slots = key.shape[1]
    lane = iota((slots, META), 1)
    meta = jnp.where(lane == 0, column_of(inside) + 1, 0).astype(F32).astype(BF16)
    owner = lax.div(key + CT_DEV, CT_DEV)
    pair = jnp.where(iota((8, slots), 0) == 0, owner, inside).astype(F32)
    index = jnp.concatenate([jnp.zeros((8, META - slots), F32), pair], axis=1)
    index += pieces(iota((8, META), 1), total(left * left))
    prods = backward(held_ref, rows, left, copies)
    tile = prods.shape[1]
    out = dot(place, jnp.concatenate([prods, meta], axis=1), 1, 0)
    out = out.reshape(npath, limit, width)
    tail = out[:, :, tile:] + jnp.broadcast_to(index[None], (npath, limit, META))
    send_ref[...] = jnp.concatenate([out[:, :, :tile], tail], axis=2).astype(BF16)


def first_owner_kernel(recv_ref, send_ref, own_ref, scal_ref):
    npath, limit, width = recv_ref.shape
    rows = npath * limit
    tile = width - META
    recv = recv_ref[...].reshape(rows, width)
    meta = recv[:, tile:].astype(F32)
    hot = onehot(meta[:, 0:1].astype(jnp.int32) == iota((rows, CT_DEV), 1) + 1)
    own = dot(hot, recv[:, :tile], 0, 0)
    own_ref[...] = own
    scal_ref[...] = jnp.broadcast_to(sum_pieces(meta) * (1.0 / limit), scal_ref.shape)
    tail = pieces(iota((rows, META), 1), total(own * own))
    full = jnp.concatenate([dot(hot, own.astype(BF16), 1, 0), tail], axis=1)
    send_ref[...] = full.astype(BF16).reshape(npath, limit, width)


def first_forward_kernel(table_ref, recv_ref, tiles_ref, out_ref):
    npath, limit, width = recv_ref.shape
    tile = width - META
    row_tiles = out_ref.shape[0]
    slot_rows, cols, count = slots_of(table_ref)
    place = placement(cols, count, npath, limit)[0]
    recv = recv_ref[...].reshape(npath * limit, width)
    picked = dot(place, recv[:, :tile], 0, 0)
    norm = sum_pieces(recv[:, tile:].astype(F32)) * (1.0 / limit)
    acc = forward(tiles_ref, slot_rows, picked, row_tiles, True)
    out_ref[...] = jnp.concatenate([acc, jnp.broadcast_to(norm, (row_tiles, META))], axis=1)


def spread(value):
    return jnp.broadcast_to(value, (1, META))


def second_kernel(
    table_ref, part_ref, other_ref, scal_ref, tiles_ref,
    send_ref, left_ref, image_ref, out_scal_ref,
):
    npath = send_ref.shape[0]
    tile = left_ref.shape[1]
    sums = part_ref[...] + other_ref[...]
    beta_sq = scal_ref[0:1, 0:1] + EPS
    beta = jnp.sqrt(beta_sq)
    norm = sums[0:1, tile : tile + 1]
    alpha_sq = norm / beta_sq + EPS
    alpha = jnp.sqrt(alpha_sq)
    data = data_of(table_ref)
    image = sums[:, :tile] / (beta * alpha)
    left = image - (alpha / beta) * data
    image_ref[...] = image
    left_ref[...] = left
    out_scal_ref[...] = jnp.zeros_like(out_scal_ref)
    out_scal_ref[0:1, :] = spread(beta)
    out_scal_ref[1:2, :] = spread(alpha)
    out_scal_ref[2:3, :] = spread(norm / (beta_sq * alpha_sq))
    prods = backward(tiles_ref, slots_of(table_ref)[0], left)
    for q in range(npath):
        send_ref[q] = prods


def second_forward_kernel(
    table_ref, recv_ref, index_ref, own_ref, scal_ref, tiles_ref,
    part_ref, next_ref,
):
    npath, slots, tile = recv_ref.shape
    row_tiles = part_ref.shape[0]
    group = max(1, tile // slots)
    me = lax.axis_index("path")
    rows, cols, count = slots_of(table_ref)
    live = iota((1, slots), 1) < count
    wanted = column_of(jnp.where(live, cols, -2 * CT_DEV))
    wanted = jnp.concatenate([iota((CT_DEV, 1), 0) + me * CT_DEV, wanted], axis=0).astype(F32)
    acc = jnp.zeros((CT_DEV + slots, tile), F32)
    for b in range(npath // group):
        keys = []
        for q in range(b * group, (b + 1) * group):
            meta = index_ref[q, :, tile:].astype(F32)
            owner, inside = meta[0:1, META - slots :], meta[1:2, META - slots :]
            keys.append((owner - 1.0) * CT_DEV + jnp.where(owner > 0.5, inside, 0.0))
        keys = jnp.concatenate(keys, axis=1)
        block = recv_ref[b * group : (b + 1) * group].reshape(group * slots, tile)
        acc += dot(onehot(wanted == keys), block, 1, 0)
    own, picked = acc[:CT_DEV], acc[CT_DEV:]
    next_ref[...] = own
    before = own_ref[...] / (scal_ref[0:1, 0:1] * scal_ref[1:2, 0:1])
    lane = iota((row_tiles, META), 1)
    tail = jnp.where(lane == 0, total(own * own), jnp.where(lane == 1, total(own * before), 0.0))
    image = forward(tiles_ref, rows, picked, row_tiles, False)
    part_ref[...] = jnp.concatenate([image, tail], axis=1)


def third_kernel(part_ref, other_ref, left_ref, image_ref, send_ref, next_ref):
    npath = send_ref.shape[0]
    tile = left_ref.shape[1]
    sums = part_ref[...] + other_ref[...]
    z, g, u = sums[:, :tile], image_ref[...], left_ref[...]
    next_ref[...] = z
    values = [total(a * b) for a, b in ((u, u), (z, z), (z, g), (z, u), (g, g), (g, u))]
    values += [sums[0:1, tile : tile + 1], sums[0:1, tile + 1 : tile + 2]]
    lane = iota((1, META), 1)
    message = jnp.concatenate([pieces(lane, v) for v in values], axis=0).astype(BF16)
    for q in range(npath):
        send_ref[q] = message


def final_kernel(
    total_rows, recv_ref, next_ref, left_ref, image_ref, own0_ref, own1_ref, scal_ref,
    solution_ref, out_ref,
):
    sums = jnp.sum(recv_ref[...].astype(F32), axis=0)
    uu, zz, zg, zu, gg, gu, yy, yv = [sum_pieces(sums[k : k + 1]) for k in range(8)]
    beta0, alpha0, vv = [scal_ref[k : k + 1, 0:1] for k in range(3)]
    beta1_sq = uu + EPS
    beta1 = jnp.sqrt(beta1_sq)
    alpha1 = jnp.sqrt(jnp.maximum(yy / beta1_sq - 2.0 * yv + beta1_sq * vv, 0.0) + EPS)
    a, b, c = 1.0 / (beta1 * alpha1), -beta1 / alpha1, -alpha1 / beta1
    norm = a * a * zz + b * b * gg + c * c * uu + 2.0 * (a * b * zg + a * c * zu + b * c * gu)
    beta2 = jnp.sqrt(jnp.maximum(norm, 0.0) + EPS)
    rho1 = jnp.sqrt(alpha0 * alpha0 + beta1 * beta1)
    cosine, sine = alpha0 / rho1, beta1 / rho1
    theta = sine * alpha1
    rhobar = -cosine * alpha1
    phi1, phibar = cosine * beta0, sine * beta0
    rho2 = jnp.sqrt(rhobar * rhobar + beta2 * beta2)
    phi2 = rhobar / rho2 * phibar
    right0 = own0_ref[...] / (beta0 * alpha0)
    right1 = (own1_ref[...] / beta1 - beta1 * right0) / alpha1
    search = right1 - (theta / rho1) * right0
    answer = (phi1 / rho1) * right0 + (phi2 / rho2) * search
    store_pairs(solution_ref, answer, answer.shape[0])
    left = a * next_ref[...] + b * image_ref[...] + c * left_ref[...]
    left = left * (total_rows**0.5 / beta2)
    store_pairs(out_ref, left, left.shape[0])


def call(kernel, ins, outs, scratch=(), flops=0, moved=0, room=LIMIT):
    shapes = [jax.ShapeDtypeStruct(s, d) for s, d in outs]
    return pl.pallas_call(
        kernel,
        in_specs=ins,
        out_specs=[VMEM] * len(outs),
        out_shape=shapes,
        scratch_shapes=scratch,
        compiler_params=pltpu.CompilerParams(vmem_limit_bytes=room),
        cost_estimate=pl.CostEstimate(flops=flops, bytes_accessed=moved, transcendentals=0),
    )


def on_device(tiles, tile_rows, tile_cols, tile_counts, data):
    slots, tile, _ = tiles.shape
    row_tiles = data.shape[0] // tile
    npath = lax.axis_size("path")
    limit = max(2, max(slots // 8, (slots + npath - 1) // npath))
    named = jnp.concatenate([tile_cols, tile_rows, jnp.broadcast_to(tile_counts, (META,))])
    named = jnp.pad(named.astype(F32), (0, 8 * META - named.shape[0]))
    table = jnp.concatenate([data, named]).reshape(-1, META)
    held = [pltpu.VMEM(tiles.shape, tiles.dtype), pltpu.SemaphoreType.DMA((CHUNKS,))]
    payload = ((npath, limit, tile + META), BF16)
    scal = ((8, META), F32)
    own_shape = ((CT_DEV, tile), F32)
    left_shape = ((row_tiles, tile), F32)
    part_shape = ((row_tiles, tile + META), F32)
    work = dict(flops=2 * 8 * tiles.size, moved=2 * tiles.size)

    def swap(x):
        return lax.all_to_all(x, "path", 0, 0, tiled=True)

    def other_half(x):
        return lax.ppermute(x, "mp", [(0, 1), (1, 0)])

    send, tiles = call(
        first_kernel,
        [VMEM, HBM],
        [payload, (tiles.shape, tiles.dtype)],
        scratch=held[1:],
        room=FIRST_LIMIT,
        **work,
    )(table, tiles)
    index = swap(send)
    send, own0, scal0 = call(first_owner_kernel, [VMEM], [payload, own_shape, scal])(index)
    recv = swap(send)
    (part,) = call(first_forward_kernel, [VMEM] * 3, [part_shape], **work)(
        table, recv, tiles
    )
    send, left, image, scal1 = call(
        second_kernel,
        [VMEM] * 5,
        [((npath, slots, tile), BF16), left_shape, left_shape, scal],
        **work,
    )(table, part, other_half(part), scal0, tiles)
    recv = swap(send)
    part, own1 = call(
        second_forward_kernel, [VMEM] * 6, [part_shape, own_shape], **work
    )(table, recv, index, own0, scal1, tiles)
    send, mixed = call(third_kernel, [VMEM] * 4, [((npath, 8, META), BF16), left_shape])(
        part, other_half(part), left, image
    )
    recv = swap(send)
    total_rows = row_tiles * tile * npath

    def last(*refs):
        final_kernel(total_rows, *refs)

    solution, left = call(
        last, [VMEM] * 7, [((CT_DEV * 2, tile // 2), F32), ((row_tiles * 2, tile // 2), F32)]
    )(recv, mixed, left, image, own0, own1, scal1)
    return solution.reshape(-1), left.reshape(-1)


def solution(mesh):
    placed = (
        P(("path", "mp"), None, None),
        P(("path", "mp")),
        P(("path", "mp")),
        P(("path", "mp")),
        P(("period", "path")),
    )
    return jax.shard_map(
        on_device,
        mesh=mesh,
        in_specs=placed,
        out_specs=(P(("period", "path", "mp")), P(("period", "path"))),
        check_vma=False,
    )
```

```python
import jax
import jax.numpy as jnp
from jax import lax
from jax.experimental import pallas as pl
from jax.experimental.pallas import tpu as pltpu
from jax.sharding import PartitionSpec as P

CT_DEV = 32
EPS = 1e-12
CHUNKS = 8
META = 128
LIMIT = 12 << 20
FIRST_LIMIT = 40 << 20
F32 = jnp.float32
BF16 = jnp.bfloat16
VMEM = pl.BlockSpec(memory_space=pltpu.VMEM)
HBM = pl.BlockSpec(memory_space=pltpu.HBM)


def iota(shape, dim):
    return lax.broadcasted_iota(jnp.int32, shape, dim)


def onehot(mask):
    return jnp.where(mask, 1.0, 0.0).astype(BF16)


def dot(a, b, ca, cb):
    return lax.dot_general(a, b, (((ca,), (cb,)), ((), ())), preferred_element_type=F32)


def total(x):
    return jnp.sum(jnp.sum(x, axis=1, keepdims=True), axis=0, keepdims=True)


def load_pairs(ref, rows):
    return jnp.concatenate(
        [ref[pl.ds(0, rows, stride=2), :], ref[pl.ds(1, rows, stride=2), :]], axis=1
    )


def store_pairs(ref, value, rows):
    half = value.shape[1] // 2
    ref[pl.ds(0, rows, stride=2), :] = value[:, :half]
    ref[pl.ds(1, rows, stride=2), :] = value[:, half:]


def pieces(lane, value):
    high = value.astype(BF16).astype(F32)
    rest = value - high
    middle = rest.astype(BF16).astype(F32)
    low = rest - middle
    return jnp.where(lane == 1, high, jnp.where(lane == 2, middle, jnp.where(lane == 3, low, 0.0)))


def sum_pieces(meta):
    lane = iota(meta.shape, 1)
    return total(jnp.where((lane >= 1) & (lane <= 3), meta, 0.0))


def split(x):
    high = x.astype(BF16)
    low = (x - high.astype(F32)).astype(BF16)
    return jnp.concatenate([high, low], axis=0)


def fold(x):
    half = x.shape[0] // 2
    return x[:half] + x[half:]


def data_of(table_ref):
    return load_pairs(table_ref.at[: table_ref.shape[0] - 8], (table_ref.shape[0] - 8) // 2)


def slots_of(table_ref):
    base = table_ref.shape[0] - 8
    slots = META // 2
    both = table_ref[base : base + 1, :].astype(jnp.int32)
    count = table_ref[base + 1 : base + 2, 0:1].astype(jnp.int32)
    return both[:, slots:], both[:, :slots], count


def column_of(row):
    n = row.shape[1]
    return jnp.sum(jnp.where(iota((n, n), 0) == iota((n, n), 1), row, 0), axis=1, keepdims=True)


def placement(cols, count, npath, limit):
    slots = cols.shape[1]
    owner = lax.div(cols, CT_DEV)
    inside = cols - owner * CT_DEV
    owner_col = column_of(owner)
    earlier = iota((slots, slots), 0) < iota((slots, slots), 1)
    same = (owner_col == owner) & earlier
    rank = jnp.sum(jnp.where(same, 1, 0), axis=0, keepdims=True)
    live = iota(cols.shape, 1) < count
    target = jnp.where(live, owner * limit + rank, -1)
    place = onehot(iota((npath * limit, slots), 0) == target)
    return place, inside


def start_tiles(tiles_ref, held, sems):
    step = held.shape[0] // CHUNKS
    copies = []
    for k in range(CHUNKS):
        part = pl.ds(k * step, step)
        copies.append(pltpu.make_async_copy(tiles_ref.at[part], held.at[part], sems.at[k]))
        copies[-1].start()
    return copies


def backward(held, rows, left, copies=None):
    slots, tile = held.shape[0], held.shape[1]
    row_tiles = left.shape[0]
    row_hot = onehot(iota((row_tiles, slots), 0) == rows)
    both = split(left)
    high = dot(row_hot, both[:row_tiles], 0, 0)
    low = dot(row_hot, both[row_tiles:], 0, 0)
    step = slots // CHUNKS
    sub = iota((2 * step, tile), 0)
    out = []
    for k in range(CHUNKS):
        if copies is not None:
            copies[k].wait()
        part = slice(k * step, (k + 1) * step)
        block = jnp.concatenate([high[part], low[part]], axis=0)
        acc = jnp.zeros((2 * step, tile), F32)
        for i in range(step):
            mine = (sub == i) | (sub == i + step)
            acc += dot(jnp.where(mine, block, 0.0).astype(BF16), held[k * step + i], 1, 0)
        out.append(fold(acc).astype(BF16))
    return jnp.concatenate(out, axis=0)


def forward(held, rows, picked, row_tiles):
    slots, tile = held.shape[0], held.shape[1]
    row_hot = jnp.where(iota((row_tiles, slots), 0) == rows, 1.0, 0.0)
    acc = jnp.zeros((row_tiles, tile), F32)
    for s in range(slots):
        lhs = row_hot[:, s : s + 1] * picked[s : s + 1, :]
        acc += dot(lhs.astype(BF16), held[s], 1, 1)
    return acc


def first_kernel(table_ref, tiles_ref, send_ref, held_ref, sems):
    npath, limit, width = send_ref.shape
    copies = start_tiles(tiles_ref, held_ref, sems)
    left = data_of(table_ref)
    rows, cols, count = slots_of(table_ref)
    place, inside = placement(cols, count, npath, limit)
    slots = cols.shape[1]
    meta = jnp.where(iota((slots, META), 1) == 0, column_of(inside) + 1, 0)
    prods = backward(held_ref, rows, left, copies)
    tile = prods.shape[1]
    terms = jnp.concatenate([prods, meta.astype(F32).astype(BF16)], axis=1)
    out = dot(place, terms, 1, 0)
    lane = iota((1, META), 1)
    sent = out[:, :tile]
    extra = pieces(lane, total(left * left)) + pieces(lane - 3, total(sent * sent))
    full = jnp.concatenate([sent, out[:, tile:] + extra], axis=1)
    send_ref[...] = full.astype(BF16).reshape(npath, limit, width)


def hot_of(meta):
    return onehot(meta[:, 0:1].astype(jnp.int32) == iota((meta.shape[0], CT_DEV), 1) + 1)


def first_owner_kernel(recv_ref, send_ref, own_ref, scal_ref):
    npath, limit, width = recv_ref.shape
    tile = width - META
    recv = recv_ref[...].reshape(npath * limit, width)
    meta = recv[:, tile:].astype(F32)
    hot = hot_of(meta)
    own = dot(hot, recv[:, :tile], 0, 0)
    own_ref[...] = own
    per = jnp.sum(meta, axis=0, keepdims=True) * (1.0 / limit)
    scal_ref[...] = jnp.zeros_like(scal_ref)
    scal_ref[0:1, :] = jnp.broadcast_to(sum_pieces(per), (1, META))
    lane = iota(per.shape, 1)
    guess = jnp.sum(jnp.where((lane >= 4) & (lane <= 6), per, 0.0), axis=1, keepdims=True)
    scal_ref[1:2, :] = jnp.broadcast_to(guess, (1, META))
    send_ref[...] = dot(hot, own.astype(BF16), 1, 0).astype(BF16).reshape(npath, limit, tile)


def forward_kernel(table_ref, recv_ref, tail_ref, tiles_ref, part_ref):
    npath, limit, tile = recv_ref.shape
    row_tiles = part_ref.shape[0]
    rows, cols, count = slots_of(table_ref)
    place, _ = placement(cols, count, npath, limit)
    picked = dot(place, recv_ref[...].reshape(npath * limit, tile), 0, 0)
    part_ref[:, :tile] = forward(tiles_ref, rows, picked, row_tiles)
    part_ref[:, tile:] = tail_ref[...]


def second_kernel(
    table_ref, part_ref, other_ref, scal_ref, tiles_ref, send_ref, image_ref, gamma_ref
):
    npath, limit, tile = send_ref.shape
    sums = part_ref[...] + other_ref[...]
    image = sums[:, :tile]
    gamma = sums[1:2, tile : tile + 1] / (scal_ref[0:1, 0:1] + EPS)
    image_ref[...] = image
    gamma_ref[...] = jnp.broadcast_to(gamma, gamma_ref.shape)
    rows, cols, count = slots_of(table_ref)
    place, _ = placement(cols, count, npath, limit)
    prods = backward(tiles_ref, rows, image - gamma * data_of(table_ref))
    send_ref[...] = dot(place, prods, 1, 0).astype(BF16).reshape(npath, limit, tile)


def second_owner_kernel(recv_ref, index_ref, own_ref, send_ref, next_ref, scal_ref):
    npath, limit, tile = recv_ref.shape
    rows = npath * limit
    hot = hot_of(index_ref[:, :, tile:].reshape(rows, META).astype(F32))
    own = dot(hot, recv_ref[...].reshape(rows, tile), 0, 0)
    next_ref[...] = own
    before = own_ref[...]
    scal_ref[...] = jnp.zeros_like(scal_ref)
    for k, value in enumerate((before * before, before * own, own * own)):
        scal_ref[k : k + 1, :] = jnp.broadcast_to(total(value), (1, META))
    send_ref[...] = dot(hot, own.astype(BF16), 1, 0).astype(BF16).reshape(npath, limit, tile)


def third_kernel(table_ref, part_ref, other_ref, image_ref, send_ref, next_ref):
    npath = send_ref.shape[0]
    tile = image_ref.shape[1]
    sums = part_ref[...] + other_ref[...]
    z, x, d = sums[:, :tile], image_ref[...], data_of(table_ref)
    next_ref[...] = z
    values = [total(a * b) for a, b in ((d, d), (d, x), (x, x), (d, z), (x, z), (z, z))]
    values += [sums[k : k + 1, tile : tile + 1] for k in range(3)]
    lane = iota((1, META), 1)
    lines = [pieces(lane, v) for v in values[:8]]
    lines[0] += pieces(lane - 3, values[8])
    message = jnp.concatenate(lines, axis=0).astype(BF16)
    for q in range(npath):
        send_ref[q] = message


def final_kernel(
    total_rows, table_ref, recv_ref, next_ref, image_ref, own0_ref, own1_ref, gamma_ref,
    solution_ref, out_ref,
):
    sums = jnp.sum(recv_ref[...].astype(F32), axis=0)
    dd, dx, xx, dz, xz, zz, vv, vy = [sum_pieces(sums[k : k + 1]) for k in range(8)]
    lane = iota((1, META), 1)
    yy = total(jnp.where((lane >= 4) & (lane <= 6), sums[0:1], 0.0))
    beta0_sq = dd + EPS
    beta0 = jnp.sqrt(beta0_sq)
    alpha0_sq = vv / beta0_sq + EPS
    alpha0 = jnp.sqrt(alpha0_sq)
    scale0 = 1.0 / (beta0 * alpha0)
    beta1_sq = xx - alpha0_sq * (2.0 * dx - alpha0_sq * dd)
    beta1_sq = (jnp.sqrt(jnp.maximum(beta1_sq, 0.0)) * scale0) ** 2 + EPS
    beta1 = jnp.sqrt(beta1_sq)
    kappa = gamma_ref[0:1, 0:1] - alpha0_sq - beta1_sq
    scale1 = scale0 / beta1
    alpha1_sq = jnp.maximum(yy + kappa * (2.0 * vy + kappa * vv), 0.0)
    alpha1_sq = (jnp.sqrt(alpha1_sq) * scale1) ** 2 + EPS
    alpha1 = jnp.sqrt(alpha1_sq)
    scale2 = scale1 / alpha1
    lam, mu = kappa - alpha1_sq, alpha1_sq * alpha0_sq
    norm = zz + lam * lam * xx + mu * mu * dd + 2.0 * (lam * xz + mu * dz + lam * mu * dx)
    beta2 = jnp.sqrt((jnp.sqrt(jnp.maximum(norm, 0.0)) * scale2) ** 2 + EPS)
    rho1 = jnp.sqrt(alpha0_sq + beta1_sq)
    cosine, sine = alpha0 / rho1, beta1 / rho1
    theta = sine * alpha1
    rhobar = -cosine * alpha1
    phi1, phibar = cosine * beta0, sine * beta0
    rho2 = jnp.sqrt(rhobar * rhobar + beta2 * beta2)
    phi2 = rhobar / rho2 * phibar
    right0 = own0_ref[...] * scale0
    right1 = (own1_ref[...] + kappa * own0_ref[...]) * scale2
    search = right1 - (theta / rho1) * right0
    answer = (phi1 / rho1) * right0 + (phi2 / rho2) * search
    store_pairs(solution_ref, answer, answer.shape[0])
    left = (next_ref[...] + lam * image_ref[...] + mu * data_of(table_ref)) * scale2
    left = left * (total_rows**0.5 / beta2)
    store_pairs(out_ref, left, left.shape[0])


def call(kernel, ins, outs, scratch=(), flops=0, moved=0, room=LIMIT):
    shapes = [jax.ShapeDtypeStruct(s, d) for s, d in outs]
    return pl.pallas_call(
        kernel,
        in_specs=ins,
        out_specs=[VMEM] * len(outs),
        out_shape=shapes,
        scratch_shapes=scratch,
        compiler_params=pltpu.CompilerParams(vmem_limit_bytes=room),
        cost_estimate=pl.CostEstimate(flops=flops, bytes_accessed=moved, transcendentals=0),
    )


def on_device(tiles, tile_rows, tile_cols, tile_counts, data):
    slots, tile, _ = tiles.shape
    row_tiles = data.shape[0] // tile
    npath = lax.axis_size("path")
    limit = max(2, max(slots // 8, (slots + npath - 1) // npath))
    named = jnp.concatenate([tile_cols, tile_rows, jnp.broadcast_to(tile_counts, (META,))])
    named = jnp.pad(named.astype(F32), (0, 8 * META - named.shape[0]))
    table = jnp.concatenate([data, named]).reshape(-1, META)
    payload = ((npath, limit, tile), BF16)
    scal = ((8, META), F32)
    own_shape = ((CT_DEV, tile), F32)
    left_shape = ((row_tiles, tile), F32)
    part_shape = ((row_tiles, tile + META), F32)
    work = dict(flops=2 * 8 * tiles.size, moved=2 * tiles.size)

    def swap(x):
        return lax.all_to_all(x, "path", 0, 0, tiled=True)

    def other_half(x):
        return lax.ppermute(x, "mp", [(0, 1), (1, 0)])

    send, tiles = call(
        first_kernel,
        [VMEM, HBM],
        [((npath, limit, tile + META), BF16), (tiles.shape, tiles.dtype)],
        scratch=[pltpu.SemaphoreType.DMA((CHUNKS,))],
        room=FIRST_LIMIT,
        **work,
    )(table, tiles)
    index = swap(send)
    send, own0, scal0 = call(first_owner_kernel, [VMEM], [payload, own_shape, scal])(index)
    pass_forward = call(forward_kernel, [VMEM] * 4, [part_shape], **work)
    (part,) = pass_forward(table, swap(send), scal0, tiles)
    send, image, gamma = call(second_kernel, [VMEM] * 5, [payload, left_shape, scal], **work)(
        table, part, other_half(part), scal0, tiles
    )
    send, own1, scal1 = call(second_owner_kernel, [VMEM] * 3, [payload, own_shape, scal])(
        swap(send), index, own0
    )
    (part,) = pass_forward(table, swap(send), scal1, tiles)
    send, mixed = call(third_kernel, [VMEM] * 4, [((npath, 8, META), BF16), left_shape])(
        table, part, other_half(part), image
    )
    total_rows = row_tiles * tile * npath

    def last(*refs):
        final_kernel(total_rows, *refs)

    solution, left = call(
        last, [VMEM] * 7, [((CT_DEV * 2, tile // 2), F32), ((row_tiles * 2, tile // 2), F32)]
    )(table, swap(send), mixed, image, own0, own1, gamma)
    return solution.reshape(-1), left.reshape(-1)


def solution(mesh):
    placed = (
        P(("path", "mp"), None, None),
        P(("path", "mp")),
        P(("path", "mp")),
        P(("path", "mp")),
        P(("period", "path")),
    )
    return jax.shard_map(
        on_device,
        mesh=mesh,
        in_specs=placed,
        out_specs=(P(("period", "path", "mp")), P(("period", "path"))),
        check_vma=False,
    )
```

```python
import jax
import jax.numpy as jnp
from jax import lax
from jax.experimental import pallas as pl
from jax.experimental.pallas import tpu as pltpu
from jax.sharding import PartitionSpec as P

CT_DEV = 32
EPS = 1e-12
CHUNKS = 8
META = 128
LIMIT = 12 << 20
FIRST_LIMIT = 40 << 20
F32 = jnp.float32
BF16 = jnp.bfloat16
VMEM = pl.BlockSpec(memory_space=pltpu.VMEM)
HBM = pl.BlockSpec(memory_space=pltpu.HBM)


def iota(shape, dim):
    return lax.broadcasted_iota(jnp.int32, shape, dim)


def onehot(mask):
    return jnp.where(mask, 1.0, 0.0).astype(BF16)


def dot(a, b, ca, cb):
    return lax.dot_general(a, b, (((ca,), (cb,)), ((), ())), preferred_element_type=F32)


def total(x):
    return jnp.sum(jnp.sum(x, axis=1, keepdims=True), axis=0, keepdims=True)


def load_pairs(ref, rows):
    return jnp.concatenate(
        [ref[pl.ds(0, rows, stride=2), :], ref[pl.ds(1, rows, stride=2), :]], axis=1
    )


def store_pairs(ref, value, rows):
    half = value.shape[1] // 2
    ref[pl.ds(0, rows, stride=2), :] = value[:, :half]
    ref[pl.ds(1, rows, stride=2), :] = value[:, half:]


def pieces(lane, value):
    high = value.astype(BF16).astype(F32)
    rest = value - high
    middle = rest.astype(BF16).astype(F32)
    low = rest - middle
    return jnp.where(lane == 1, high, jnp.where(lane == 2, middle, jnp.where(lane == 3, low, 0.0)))


def sum_pieces(meta):
    lane = iota(meta.shape, 1)
    return total(jnp.where((lane >= 1) & (lane <= 3), meta, 0.0))


def split(x):
    high = x.astype(BF16)
    low = (x - high.astype(F32)).astype(BF16)
    return jnp.concatenate([high, low], axis=0)


def fold(x):
    half = x.shape[0] // 2
    return x[:half] + x[half:]


def data_of(table_ref):
    return load_pairs(table_ref.at[: table_ref.shape[0] - 8], (table_ref.shape[0] - 8) // 2)


def slots_of(table_ref):
    base = table_ref.shape[0] - 8
    slots = META // 2
    both = table_ref[base : base + 1, :].astype(jnp.int32)
    count = table_ref[base + 1 : base + 2, 0:1].astype(jnp.int32)
    return both[:, slots:], both[:, :slots], count


def column_of(row):
    n = row.shape[1]
    return jnp.sum(jnp.where(iota((n, n), 0) == iota((n, n), 1), row, 0), axis=1, keepdims=True)


def placement(cols, count, npath, limit):
    slots = cols.shape[1]
    owner = lax.div(cols, CT_DEV)
    inside = cols - owner * CT_DEV
    owner_col = column_of(owner)
    earlier = iota((slots, slots), 0) < iota((slots, slots), 1)
    same = (owner_col == owner) & earlier
    rank = jnp.sum(jnp.where(same, 1, 0), axis=0, keepdims=True)
    live = iota(cols.shape, 1) < count
    target = jnp.where(live, owner * limit + rank, -1)
    place = onehot(iota((npath * limit, slots), 0) == target)
    return place, inside


def start_tiles(tiles_ref, held, sems):
    step = held.shape[0] // CHUNKS
    copies = []
    for k in range(CHUNKS):
        part = pl.ds(k * step, step)
        copies.append(pltpu.make_async_copy(tiles_ref.at[part], held.at[part], sems.at[k]))
        copies[-1].start()
    return copies


def backward(held, rows, left, copies=None):
    slots, tile = held.shape[0], held.shape[1]
    row_tiles = left.shape[0]
    row_hot = onehot(iota((row_tiles, slots), 0) == rows)
    both = split(left)
    high = dot(row_hot, both[:row_tiles], 0, 0)
    low = dot(row_hot, both[row_tiles:], 0, 0)
    step = slots // CHUNKS
    sub = iota((2 * step, tile), 0)
    out = []
    for k in range(CHUNKS):
        if copies is not None:
            copies[k].wait()
        part = slice(k * step, (k + 1) * step)
        block = jnp.concatenate([high[part], low[part]], axis=0)
        acc = jnp.zeros((2 * step, tile), F32)
        for i in range(step):
            mine = (sub == i) | (sub == i + step)
            acc += dot(jnp.where(mine, block, 0.0).astype(BF16), held[k * step + i], 1, 0)
        out.append(fold(acc).astype(BF16))
    return jnp.concatenate(out, axis=0)


def forward(held, rows, picked, row_tiles):
    slots, tile = held.shape[0], held.shape[1]
    row_hot = jnp.where(iota((row_tiles, slots), 0) == rows, 1.0, 0.0)
    acc = jnp.zeros((row_tiles, tile), F32)
    for s in range(slots):
        lhs = row_hot[:, s : s + 1] * picked[s : s + 1, :]
        acc += dot(lhs.astype(BF16), held[s], 1, 1)
    return acc


def first_kernel(table_ref, tiles_ref, send_ref, held_ref, place_ref, sems):
    npath, limit, width = send_ref.shape
    copies = start_tiles(tiles_ref, held_ref, sems)
    left = data_of(table_ref)
    rows, cols, count = slots_of(table_ref)
    place, inside = placement(cols, count, npath, limit)
    place_ref[...] = place
    slots = cols.shape[1]
    meta = jnp.where(iota((slots, META), 1) == 0, column_of(inside) + 1, 0)
    prods = backward(held_ref, rows, left, copies)
    tile = prods.shape[1]
    terms = jnp.concatenate([prods, meta.astype(F32).astype(BF16)], axis=1)
    out = dot(place, terms, 1, 0)
    lane = iota((1, META), 1)
    sent = out[:, :tile]
    extra = pieces(lane, total(left * left)) + pieces(lane - 3, total(sent * sent))
    full = jnp.concatenate([sent, out[:, tile:] + extra], axis=1)
    send_ref[...] = full.astype(BF16).reshape(npath, limit, width)


def hot_of(meta):
    return onehot(meta[:, 0:1].astype(jnp.int32) == iota((meta.shape[0], CT_DEV), 1) + 1)


def first_owner_kernel(recv_ref, send_ref, own_ref, scal_ref):
    npath, limit, width = recv_ref.shape
    tile = width - META
    recv = recv_ref[...].reshape(npath * limit, width)
    meta = recv[:, tile:].astype(F32)
    hot = hot_of(meta)
    own = dot(hot, recv[:, :tile], 0, 0)
    own_ref[...] = own
    per = jnp.sum(meta, axis=0, keepdims=True) * (1.0 / limit)
    scal_ref[...] = jnp.zeros_like(scal_ref)
    scal_ref[0:1, :] = jnp.broadcast_to(sum_pieces(per), (1, META))
    lane = iota(per.shape, 1)
    guess = jnp.sum(jnp.where((lane >= 4) & (lane <= 6), per, 0.0), axis=1, keepdims=True)
    scal_ref[1:2, :] = jnp.broadcast_to(guess, (1, META))
    send_ref[...] = dot(hot, own.astype(BF16), 1, 0).astype(BF16).reshape(npath, limit, tile)


def forward_kernel(table_ref, place_ref, recv_ref, tail_ref, tiles_ref, part_ref):
    npath, limit, tile = recv_ref.shape
    row_tiles = part_ref.shape[0]
    rows = slots_of(table_ref)[0]
    picked = dot(place_ref[...], recv_ref[...].reshape(npath * limit, tile), 0, 0)
    part_ref[:, :tile] = forward(tiles_ref, rows, picked, row_tiles)
    part_ref[:, tile:] = tail_ref[...]


def second_kernel(
    table_ref, place_ref, part_ref, other_ref, scal_ref, tiles_ref,
    send_ref, image_ref, gamma_ref,
):
    npath, limit, tile = send_ref.shape
    sums = part_ref[...] + other_ref[...]
    image = sums[:, :tile]
    gamma = sums[1:2, tile : tile + 1] / (scal_ref[0:1, 0:1] + EPS)
    image_ref[...] = image
    gamma_ref[...] = jnp.broadcast_to(gamma, gamma_ref.shape)
    rows = slots_of(table_ref)[0]
    prods = backward(tiles_ref, rows, image - gamma * data_of(table_ref))
    send_ref[...] = dot(place_ref[...], prods, 1, 0).astype(BF16).reshape(npath, limit, tile)


def second_owner_kernel(recv_ref, index_ref, own_ref, send_ref, next_ref, scal_ref):
    npath, limit, tile = recv_ref.shape
    rows = npath * limit
    hot = hot_of(index_ref[:, :, tile:].reshape(rows, META).astype(F32))
    own = dot(hot, recv_ref[...].reshape(rows, tile), 0, 0)
    next_ref[...] = own
    before = own_ref[...]
    scal_ref[...] = jnp.zeros_like(scal_ref)
    for k, value in enumerate((before * before, before * own, own * own)):
        scal_ref[k : k + 1, :] = jnp.broadcast_to(total(value), (1, META))
    send_ref[...] = dot(hot, own.astype(BF16), 1, 0).astype(BF16).reshape(npath, limit, tile)


def third_kernel(table_ref, part_ref, other_ref, image_ref, send_ref, next_ref):
    npath = send_ref.shape[0]
    tile = image_ref.shape[1]
    sums = part_ref[...] + other_ref[...]
    z, x, d = sums[:, :tile], image_ref[...], data_of(table_ref)
    next_ref[...] = z
    values = [total(a * b) for a, b in ((d, d), (d, x), (x, x), (d, z), (x, z), (z, z))]
    values += [sums[k : k + 1, tile : tile + 1] for k in range(3)]
    lane = iota((1, META), 1)
    lines = [pieces(lane, v) for v in values[:8]]
    lines[0] += pieces(lane - 3, values[8])
    message = jnp.concatenate(lines, axis=0).astype(BF16)
    for q in range(npath):
        send_ref[q] = message


def final_kernel(
    total_rows, table_ref, recv_ref, next_ref, image_ref, own0_ref, own1_ref, gamma_ref,
    solution_ref, out_ref,
):
    sums = jnp.sum(recv_ref[...].astype(F32), axis=0)
    dd, dx, xx, dz, xz, zz, vv, vy = [sum_pieces(sums[k : k + 1]) for k in range(8)]
    lane = iota((1, META), 1)
    yy = total(jnp.where((lane >= 4) & (lane <= 6), sums[0:1], 0.0))
    beta0_sq = dd + EPS
    beta0 = jnp.sqrt(beta0_sq)
    alpha0_sq = vv / beta0_sq + EPS
    alpha0 = jnp.sqrt(alpha0_sq)
    scale0 = 1.0 / (beta0 * alpha0)
    beta1_sq = xx - alpha0_sq * (2.0 * dx - alpha0_sq * dd)
    beta1_sq = (jnp.sqrt(jnp.maximum(beta1_sq, 0.0)) * scale0) ** 2 + EPS
    beta1 = jnp.sqrt(beta1_sq)
    kappa = gamma_ref[0:1, 0:1] - alpha0_sq - beta1_sq
    scale1 = scale0 / beta1
    alpha1_sq = jnp.maximum(yy + kappa * (2.0 * vy + kappa * vv), 0.0)
    alpha1_sq = (jnp.sqrt(alpha1_sq) * scale1) ** 2 + EPS
    alpha1 = jnp.sqrt(alpha1_sq)
    scale2 = scale1 / alpha1
    lam, mu = kappa - alpha1_sq, alpha1_sq * alpha0_sq
    norm = zz + lam * lam * xx + mu * mu * dd + 2.0 * (lam * xz + mu * dz + lam * mu * dx)
    beta2 = jnp.sqrt((jnp.sqrt(jnp.maximum(norm, 0.0)) * scale2) ** 2 + EPS)
    rho1 = jnp.sqrt(alpha0_sq + beta1_sq)
    cosine, sine = alpha0 / rho1, beta1 / rho1
    theta = sine * alpha1
    rhobar = -cosine * alpha1
    phi1, phibar = cosine * beta0, sine * beta0
    rho2 = jnp.sqrt(rhobar * rhobar + beta2 * beta2)
    phi2 = rhobar / rho2 * phibar
    right0 = own0_ref[...] * scale0
    right1 = (own1_ref[...] + kappa * own0_ref[...]) * scale2
    search = right1 - (theta / rho1) * right0
    answer = (phi1 / rho1) * right0 + (phi2 / rho2) * search
    store_pairs(solution_ref, answer, answer.shape[0])
    left = (next_ref[...] + lam * image_ref[...] + mu * data_of(table_ref)) * scale2
    left = left * (total_rows**0.5 / beta2)
    store_pairs(out_ref, left, left.shape[0])


def call(kernel, ins, outs, scratch=(), flops=0, moved=0, room=LIMIT):
    shapes = [jax.ShapeDtypeStruct(s, d) for s, d in outs]
    return pl.pallas_call(
        kernel,
        in_specs=ins,
        out_specs=[VMEM] * len(outs),
        out_shape=shapes,
        scratch_shapes=scratch,
        compiler_params=pltpu.CompilerParams(vmem_limit_bytes=room),
        cost_estimate=pl.CostEstimate(flops=flops, bytes_accessed=moved, transcendentals=0),
    )


def on_device(tiles, tile_rows, tile_cols, tile_counts, data):
    slots, tile, _ = tiles.shape
    row_tiles = data.shape[0] // tile
    npath = lax.axis_size("path")
    limit = max(2, max(slots // 8, (slots + npath - 1) // npath))
    cells = data.shape[0] + 8 * META
    named, start = 0, data.shape[0]
    for x in (tile_cols, tile_rows, tile_counts):
        named += jnp.pad(x, (start, cells - start - x.shape[0]))
        start += x.shape[0]
    table = named.astype(F32) + jnp.pad(data, (0, cells - data.shape[0]))
    table = table.reshape(-1, META)
    payload = ((npath, limit, tile), BF16)
    scal = ((8, META), F32)
    own_shape = ((CT_DEV, tile), F32)
    left_shape = ((row_tiles, tile), F32)
    part_shape = ((row_tiles, tile + META), F32)
    work = dict(flops=2 * 8 * tiles.size, moved=2 * tiles.size)

    def swap(x):
        return lax.all_to_all(x, "path", 0, 0, tiled=True)

    def other_half(x):
        return lax.ppermute(x, "mp", [(0, 1), (1, 0)])

    send, tiles, place = call(
        first_kernel,
        [VMEM, HBM],
        [
            ((npath, limit, tile + META), BF16),
            (tiles.shape, tiles.dtype),
            ((npath * limit, slots), BF16),
        ],
        scratch=[pltpu.SemaphoreType.DMA((CHUNKS,))],
        room=FIRST_LIMIT,
        **work,
    )(table, tiles)
    index = swap(send)
    send, own0, scal0 = call(first_owner_kernel, [VMEM], [payload, own_shape, scal])(index)
    pass_forward = call(forward_kernel, [VMEM] * 5, [part_shape], **work)
    (part,) = pass_forward(table, place, swap(send), scal0, tiles)
    send, image, gamma = call(second_kernel, [VMEM] * 6, [payload, left_shape, scal], **work)(
        table, place, part, other_half(part), scal0, tiles
    )
    send, own1, scal1 = call(second_owner_kernel, [VMEM] * 3, [payload, own_shape, scal])(
        swap(send), index, own0
    )
    (part,) = pass_forward(table, place, swap(send), scal1, tiles)
    send, mixed = call(third_kernel, [VMEM] * 4, [((npath, 8, META), BF16), left_shape])(
        table, part, other_half(part), image
    )
    total_rows = row_tiles * tile * npath

    def last(*refs):
        final_kernel(total_rows, *refs)

    solution, left = call(
        last, [VMEM] * 7, [((CT_DEV * 2, tile // 2), F32), ((row_tiles * 2, tile // 2), F32)]
    )(table, swap(send), mixed, image, own0, own1, gamma)
    return solution.reshape(-1), left.reshape(-1)


def solution(mesh):
    placed = (
        P(("path", "mp"), None, None),
        P(("path", "mp")),
        P(("path", "mp")),
        P(("path", "mp")),
        P(("period", "path")),
    )
    return jax.shard_map(
        on_device,
        mesh=mesh,
        in_specs=placed,
        out_specs=(P(("period", "path", "mp")), P(("period", "path"))),
        check_vma=False,
    )
```

```python
import jax
import jax.numpy as jnp
from jax import lax
from jax.experimental import pallas as pl
from jax.experimental.pallas import tpu as pltpu
from jax.sharding import PartitionSpec as P

CT_DEV = 32
EPS = 1e-12
CHUNKS = 8
META = 128
LIMIT = 12 << 20
FIRST_LIMIT = 40 << 20
F32 = jnp.float32
BF16 = jnp.bfloat16
VMEM = pl.BlockSpec(memory_space=pltpu.VMEM)
SMEM = pl.BlockSpec(memory_space=pltpu.SMEM)
HBM = pl.BlockSpec(memory_space=pltpu.HBM)


def iota(shape, dim):
    return lax.broadcasted_iota(jnp.int32, shape, dim)


def onehot(mask):
    return jnp.where(mask, 1.0, 0.0).astype(BF16)


def dot(a, b, ca, cb):
    return lax.dot_general(a, b, (((ca,), (cb,)), ((), ())), preferred_element_type=F32)


def total(x):
    return jnp.sum(jnp.sum(x, axis=1, keepdims=True), axis=0, keepdims=True)


def load_pairs(ref, rows):
    return jnp.concatenate(
        [ref[pl.ds(0, rows, stride=2), :], ref[pl.ds(1, rows, stride=2), :]], axis=1
    )


def store_pairs(ref, value, rows):
    half = value.shape[1] // 2
    ref[pl.ds(0, rows, stride=2), :] = value[:, :half]
    ref[pl.ds(1, rows, stride=2), :] = value[:, half:]


def pieces(lane, value):
    high = value.astype(BF16).astype(F32)
    rest = value - high
    middle = rest.astype(BF16).astype(F32)
    low = rest - middle
    return jnp.where(lane == 1, high, jnp.where(lane == 2, middle, jnp.where(lane == 3, low, 0.0)))


def sum_pieces(meta):
    lane = iota(meta.shape, 1)
    return total(jnp.where((lane >= 1) & (lane <= 3), meta, 0.0))


def split(x):
    high = x.astype(BF16)
    low = (x - high.astype(F32)).astype(BF16)
    return jnp.concatenate([high, low], axis=0)


def fold(x):
    half = x.shape[0] // 2
    return x[:half] + x[half:]


def data_of(table_ref):
    return load_pairs(table_ref.at[: table_ref.shape[0] - 8], (table_ref.shape[0] - 8) // 2)


def slots_of(table_ref):
    base = table_ref.shape[0] - 8
    slots = META // 2
    both = table_ref[base : base + 1, :].astype(jnp.int32)
    count = table_ref[base + 1 : base + 2, 0:1].astype(jnp.int32)
    return both[:, slots:], both[:, :slots], count


def column_of(row):
    n = row.shape[1]
    return jnp.sum(jnp.where(iota((n, n), 0) == iota((n, n), 1), row, 0), axis=1, keepdims=True)


def placement(cols, count, npath, limit):
    slots = cols.shape[1]
    owner = lax.div(cols, CT_DEV)
    inside = cols - owner * CT_DEV
    owner_col = column_of(owner)
    earlier = iota((slots, slots), 0) < iota((slots, slots), 1)
    same = (owner_col == owner) & earlier
    rank = jnp.sum(jnp.where(same, 1, 0), axis=0, keepdims=True)
    live = iota(cols.shape, 1) < count
    target = jnp.where(live, owner * limit + rank, -1)
    place = onehot(iota((npath * limit, slots), 0) == target)
    return place, inside


def start_tiles(tiles_ref, held, sems):
    step = held.shape[0] // CHUNKS
    copies = []
    for k in range(CHUNKS):
        part = pl.ds(k * step, step)
        copies.append(pltpu.make_async_copy(tiles_ref.at[part], held.at[part], sems.at[k]))
        copies[-1].start()
    return copies


def backward_parts(held, rows, left, copies=None):
    slots, tile = held.shape[0], held.shape[1]
    row_tiles = left.shape[0]
    row_hot = onehot(iota((row_tiles, slots), 0) == rows)
    both = split(left)
    high = dot(row_hot, both[:row_tiles], 0, 0)
    low = dot(row_hot, both[row_tiles:], 0, 0)
    step = slots // CHUNKS
    sub = iota((2 * step, tile), 0)
    for k in range(CHUNKS):
        if copies is not None:
            copies[k].wait()
        part = slice(k * step, (k + 1) * step)
        block = jnp.concatenate([high[part], low[part]], axis=0)
        acc = jnp.zeros((2 * step, tile), F32)
        for i in range(step):
            mine = (sub == i) | (sub == i + step)
            acc += dot(jnp.where(mine, block, 0.0).astype(BF16), held[k * step + i], 1, 0)
        yield fold(acc).astype(BF16)


def backward(held, rows, left):
    return jnp.concatenate(list(backward_parts(held, rows, left)), axis=0)


def forward(held, rows, picked, row_tiles):
    slots, tile = held.shape[0], held.shape[1]
    row_hot = jnp.where(iota((row_tiles, slots), 0) == rows, 1.0, 0.0)
    acc = jnp.zeros((row_tiles, tile), F32)
    for s in range(slots):
        lhs = row_hot[:, s : s + 1] * picked[s : s + 1, :]
        acc += dot(lhs.astype(BF16), held[s], 1, 1)
    return acc


def first_kernel(
    data_ref, cols_ref, rows_ref, count_ref, tiles_ref,
    send_ref, held_ref, place_ref, table_ref, cols_buf, rows_buf, sems, small,
):
    npath, limit, width = send_ref.shape
    lines = data_ref.shape[0]
    pairs = (
        (data_ref, table_ref.at[:lines]), (cols_ref, cols_buf), (rows_ref, rows_buf)
    )
    loads = [pltpu.make_async_copy(a, b, small.at[k]) for k, (a, b) in enumerate(pairs)]
    for load in loads:
        load.start()
    copies = start_tiles(tiles_ref, held_ref, sems)
    for load in loads:
        load.wait()
    named = jnp.concatenate([cols_buf[...], rows_buf[...]], axis=1).astype(F32)
    table_ref[lines:, :] = jnp.where(iota((8, META), 0) == 0, named, 1.0 * count_ref[0])
    left = data_of(table_ref)
    rows, cols, count = slots_of(table_ref)
    place, inside = placement(cols, count, npath, limit)
    place_ref[...] = place
    slots = cols.shape[1]
    meta = jnp.where(iota((slots, META), 1) == 0, column_of(inside) + 1, 0)
    meta = meta.astype(F32).astype(BF16)
    live = column_of(jnp.where(iota(cols.shape, 1) < count, 1, 0)).astype(F32)
    tile = left.shape[1]
    parts, norm = [], jnp.zeros((1, 1), F32)
    for k, part in enumerate(backward_parts(held_ref, rows, left, copies)):
        step = part.shape[0]
        kept = part.astype(F32) * live[k * step : (k + 1) * step]
        norm += total(kept * kept)
        parts.append(part)
        if k >= CHUNKS - 2:
            before = jnp.zeros(((k + 1) * step - len(parts) * step, tile), BF16)
            after = jnp.zeros((slots - (k + 1) * step, tile), BF16)
            terms = jnp.concatenate([x for x in (before, *parts, after) if x.shape[0]], axis=0)
            if k == CHUNKS - 2:
                out = dot(place, jnp.concatenate([terms, meta], axis=1), 1, 0)
            else:
                last = dot(place, terms, 1, 0)
            parts = []
    lane = iota((1, META), 1)
    extra = pieces(lane, total(left * left)) + pieces(lane - 3, norm)
    full = jnp.concatenate([out[:, :tile] + last, out[:, tile:] + extra], axis=1)
    send_ref[...] = full.astype(BF16).reshape(npath, limit, width)


def hot_of(meta):
    return onehot(meta[:, 0:1].astype(jnp.int32) == iota((meta.shape[0], CT_DEV), 1) + 1)


def first_owner_kernel(recv_ref, send_ref, own_ref, scal_ref):
    npath, limit, width = recv_ref.shape
    tile = width - META
    recv = recv_ref[...].reshape(npath * limit, width)
    meta = recv[:, tile:].astype(F32)
    hot = hot_of(meta)
    own = dot(hot, recv[:, :tile], 0, 0)
    own_ref[...] = own
    per = jnp.sum(meta, axis=0, keepdims=True) * (1.0 / limit)
    scal_ref[...] = jnp.zeros_like(scal_ref)
    scal_ref[0:1, :] = jnp.broadcast_to(sum_pieces(per), (1, META))
    lane = iota(per.shape, 1)
    guess = jnp.sum(jnp.where((lane >= 4) & (lane <= 6), per, 0.0), axis=1, keepdims=True)
    scal_ref[1:2, :] = jnp.broadcast_to(guess, (1, META))
    send_ref[...] = dot(hot, own.astype(BF16), 1, 0).astype(BF16).reshape(npath, limit, tile)


def forward_kernel(table_ref, place_ref, recv_ref, tail_ref, tiles_ref, part_ref):
    npath, limit, tile = recv_ref.shape
    row_tiles = part_ref.shape[0]
    rows = slots_of(table_ref)[0]
    picked = dot(place_ref[...], recv_ref[...].reshape(npath * limit, tile), 0, 0)
    part_ref[:, :tile] = forward(tiles_ref, rows, picked, row_tiles)
    part_ref[:, tile:] = tail_ref[...]


def second_kernel(
    table_ref, place_ref, part_ref, other_ref, scal_ref, tiles_ref,
    send_ref, image_ref, gamma_ref,
):
    npath, limit, tile = send_ref.shape
    sums = part_ref[...] + other_ref[...]
    image = sums[:, :tile]
    gamma = sums[1:2, tile : tile + 1] / (scal_ref[0:1, 0:1] + EPS)
    image_ref[...] = image
    gamma_ref[...] = jnp.broadcast_to(gamma, gamma_ref.shape)
    rows = slots_of(table_ref)[0]
    prods = backward(tiles_ref, rows, image - gamma * data_of(table_ref))
    send_ref[...] = dot(place_ref[...], prods, 1, 0).astype(BF16).reshape(npath, limit, tile)


def second_owner_kernel(recv_ref, index_ref, own_ref, send_ref, next_ref, scal_ref):
    npath, limit, tile = recv_ref.shape
    rows = npath * limit
    hot = hot_of(index_ref[:, :, tile:].reshape(rows, META).astype(F32))
    own = dot(hot, recv_ref[...].reshape(rows, tile), 0, 0)
    next_ref[...] = own
    before = own_ref[...]
    scal_ref[...] = jnp.zeros_like(scal_ref)
    for k, value in enumerate((before * before, before * own, own * own)):
        scal_ref[k : k + 1, :] = jnp.broadcast_to(total(value), (1, META))
    send_ref[...] = dot(hot, own.astype(BF16), 1, 0).astype(BF16).reshape(npath, limit, tile)


def third_kernel(table_ref, part_ref, other_ref, image_ref, send_ref, next_ref):
    npath = send_ref.shape[0]
    tile = image_ref.shape[1]
    sums = part_ref[...] + other_ref[...]
    z, x, d = sums[:, :tile], image_ref[...], data_of(table_ref)
    next_ref[...] = z
    values = [total(a * b) for a, b in ((d, d), (d, x), (x, x), (d, z), (x, z), (z, z))]
    values += [sums[k : k + 1, tile : tile + 1] for k in range(3)]
    lane = iota((1, META), 1)
    lines = [pieces(lane, v) for v in values[:8]]
    lines[0] += pieces(lane - 3, values[8])
    message = jnp.concatenate(lines, axis=0).astype(BF16)
    for q in range(npath):
        send_ref[q] = message


def final_kernel(
    total_rows, table_ref, recv_ref, next_ref, image_ref, own0_ref, own1_ref, gamma_ref,
    solution_ref, out_ref,
):
    sums = jnp.sum(recv_ref[...].astype(F32), axis=0)
    dd, dx, xx, dz, xz, zz, vv, vy = [sum_pieces(sums[k : k + 1]) for k in range(8)]
    lane = iota((1, META), 1)
    yy = total(jnp.where((lane >= 4) & (lane <= 6), sums[0:1], 0.0))
    beta0_sq = dd + EPS
    beta0 = jnp.sqrt(beta0_sq)
    alpha0_sq = vv / beta0_sq + EPS
    alpha0 = jnp.sqrt(alpha0_sq)
    scale0 = 1.0 / (beta0 * alpha0)
    beta1_sq = xx - alpha0_sq * (2.0 * dx - alpha0_sq * dd)
    beta1_sq = (jnp.sqrt(jnp.maximum(beta1_sq, 0.0)) * scale0) ** 2 + EPS
    beta1 = jnp.sqrt(beta1_sq)
    kappa = gamma_ref[0:1, 0:1] - alpha0_sq - beta1_sq
    scale1 = scale0 / beta1
    alpha1_sq = jnp.maximum(yy + kappa * (2.0 * vy + kappa * vv), 0.0)
    alpha1_sq = (jnp.sqrt(alpha1_sq) * scale1) ** 2 + EPS
    alpha1 = jnp.sqrt(alpha1_sq)
    scale2 = scale1 / alpha1
    lam, mu = kappa - alpha1_sq, alpha1_sq * alpha0_sq
    norm = zz + lam * lam * xx + mu * mu * dd + 2.0 * (lam * xz + mu * dz + lam * mu * dx)
    beta2 = jnp.sqrt((jnp.sqrt(jnp.maximum(norm, 0.0)) * scale2) ** 2 + EPS)
    rho1 = jnp.sqrt(alpha0_sq + beta1_sq)
    cosine, sine = alpha0 / rho1, beta1 / rho1
    theta = sine * alpha1
    rhobar = -cosine * alpha1
    phi1, phibar = cosine * beta0, sine * beta0
    rho2 = jnp.sqrt(rhobar * rhobar + beta2 * beta2)
    phi2 = rhobar / rho2 * phibar
    right0 = own0_ref[...] * scale0
    right1 = (own1_ref[...] + kappa * own0_ref[...]) * scale2
    search = right1 - (theta / rho1) * right0
    answer = (phi1 / rho1) * right0 + (phi2 / rho2) * search
    store_pairs(solution_ref, answer, answer.shape[0])
    left = (next_ref[...] + lam * image_ref[...] + mu * data_of(table_ref)) * scale2
    left = left * (total_rows**0.5 / beta2)
    store_pairs(out_ref, left, left.shape[0])


def call(kernel, ins, outs, scratch=(), flops=0, moved=0, room=LIMIT):
    shapes = [jax.ShapeDtypeStruct(s, d) for s, d in outs]
    return pl.pallas_call(
        kernel,
        in_specs=ins,
        out_specs=[VMEM] * len(outs),
        out_shape=shapes,
        scratch_shapes=scratch,
        compiler_params=pltpu.CompilerParams(vmem_limit_bytes=room),
        cost_estimate=pl.CostEstimate(flops=flops, bytes_accessed=moved, transcendentals=0),
    )


def on_device(tiles, tile_rows, tile_cols, tile_counts, data):
    slots, tile, _ = tiles.shape
    row_tiles = data.shape[0] // tile
    npath = lax.axis_size("path")
    limit = max(2, max(slots // 8, (slots + npath - 1) // npath))
    data = data.reshape(-1, META)
    payload = ((npath, limit, tile), BF16)
    scal = ((8, META), F32)
    own_shape = ((CT_DEV, tile), F32)
    left_shape = ((row_tiles, tile), F32)
    part_shape = ((row_tiles, tile + META), F32)
    work = dict(flops=2 * 8 * tiles.size, moved=2 * tiles.size)

    def swap(x):
        return lax.all_to_all(x, "path", 0, 0, tiled=True)

    def other_half(x):
        return lax.ppermute(x, "mp", [(0, 1), (1, 0)])

    inputs = (data, tile_cols.reshape(1, slots), tile_rows.reshape(1, slots), tile_counts, tiles)
    send, tiles, place, table = call(
        first_kernel,
        [HBM] * 3 + [SMEM, HBM],
        [
            ((npath, limit, tile + META), BF16),
            (tiles.shape, tiles.dtype),
            ((npath * limit, slots), BF16),
            ((data.shape[0] + 8, META), F32),
        ],
        scratch=[
            pltpu.VMEM((1, slots), jnp.int32),
            pltpu.VMEM((1, slots), jnp.int32),
            pltpu.SemaphoreType.DMA((CHUNKS,)),
            pltpu.SemaphoreType.DMA((3,)),
        ],
        room=FIRST_LIMIT,
        **work,
    )(*[x if x.size == 1 else pltpu.with_memory_space_constraint(x, pltpu.HBM) for x in inputs])
    index = swap(send)
    send, own0, scal0 = call(first_owner_kernel, [VMEM], [payload, own_shape, scal])(index)
    pass_forward = call(forward_kernel, [VMEM] * 5, [part_shape], **work)
    (part,) = pass_forward(table, place, swap(send), scal0, tiles)
    send, image, gamma = call(second_kernel, [VMEM] * 6, [payload, left_shape, scal], **work)(
        table, place, part, other_half(part), scal0, tiles
    )
    send, own1, scal1 = call(second_owner_kernel, [VMEM] * 3, [payload, own_shape, scal])(
        swap(send), index, own0
    )
    (part,) = pass_forward(table, place, swap(send), scal1, tiles)
    send, mixed = call(third_kernel, [VMEM] * 4, [((npath, 8, META), BF16), left_shape])(
        table, part, other_half(part), image
    )
    total_rows = row_tiles * tile * npath

    def last(*refs):
        final_kernel(total_rows, *refs)

    solution, left = call(
        last, [VMEM] * 7, [((CT_DEV * 2, tile // 2), F32), ((row_tiles * 2, tile // 2), F32)]
    )(table, swap(send), mixed, image, own0, own1, gamma)
    return solution.reshape(-1), left.reshape(-1)


def solution(mesh):
    placed = (
        P(("path", "mp"), None, None),
        P(("path", "mp")),
        P(("path", "mp")),
        P(("path", "mp")),
        P(("period", "path")),
    )
    return jax.shard_map(
        on_device,
        mesh=mesh,
        in_specs=placed,
        out_specs=(P(("period", "path", "mp")), P(("period", "path"))),
        check_vma=False,
    )
```

```python
import jax
import jax.numpy as jnp
from jax import lax
from jax.experimental import pallas as pl
from jax.experimental.pallas import tpu as pltpu
from jax.sharding import PartitionSpec as P

CT_DEV = 32
EPS = 1e-12
CHUNKS = 8
TURNED = 8
META = 128
LIMIT = 12 << 20
FIRST_LIMIT = 16 << 20
F32 = jnp.float32
BF16 = jnp.bfloat16
VMEM = pl.BlockSpec(memory_space=pltpu.VMEM)
HBM = pl.BlockSpec(memory_space=pltpu.HBM)


def iota(shape, dim):
    return lax.broadcasted_iota(jnp.int32, shape, dim)


def onehot(mask):
    return jnp.where(mask, 1.0, 0.0).astype(BF16)


def dot(a, b, ca, cb):
    return lax.dot_general(a, b, (((ca,), (cb,)), ((), ())), preferred_element_type=F32)


def total(x):
    return jnp.sum(jnp.sum(x, axis=1, keepdims=True), axis=0, keepdims=True)


def load_pairs(ref, rows):
    return jnp.concatenate(
        [ref[pl.ds(0, rows, stride=2), :], ref[pl.ds(1, rows, stride=2), :]], axis=1
    )


def store_pairs(ref, value, rows):
    half = value.shape[1] // 2
    ref[pl.ds(0, rows, stride=2), :] = value[:, :half]
    ref[pl.ds(1, rows, stride=2), :] = value[:, half:]


def pieces(lane, value):
    high = value.astype(BF16).astype(F32)
    rest = value - high
    middle = rest.astype(BF16).astype(F32)
    low = rest - middle
    return jnp.where(lane == 1, high, jnp.where(lane == 2, middle, jnp.where(lane == 3, low, 0.0)))


def sum_pieces(meta):
    lane = iota(meta.shape, 1)
    return total(jnp.where((lane >= 1) & (lane <= 3), meta, 0.0))


def split(x):
    high = x.astype(BF16)
    low = (x - high.astype(F32)).astype(BF16)
    return jnp.concatenate([high, low], axis=0)


def fold(x):
    half = x.shape[0] // 2
    return x[:half] + x[half:]


def data_of(table_ref):
    return load_pairs(table_ref.at[: table_ref.shape[0] - 8], (table_ref.shape[0] - 8) // 2)


def slots_of(table_ref):
    base = table_ref.shape[0] - 8
    slots = META // 2
    both = table_ref[base : base + 1, :].astype(jnp.int32)
    count = table_ref[base + 1 : base + 2, 0:1].astype(jnp.int32)
    return both[:, slots:], both[:, :slots], count


def column_of(row):
    n = row.shape[1]
    return jnp.sum(jnp.where(iota((n, n), 0) == iota((n, n), 1), row, 0), axis=1, keepdims=True)


def placement(cols, count, npath, limit):
    slots = cols.shape[1]
    owner = lax.div(cols, CT_DEV)
    inside = cols - owner * CT_DEV
    owner_col = column_of(owner)
    earlier = iota((slots, slots), 0) < iota((slots, slots), 1)
    same = (owner_col == owner) & earlier
    rank = jnp.sum(jnp.where(same, 1, 0), axis=0, keepdims=True)
    live = iota(cols.shape, 1) < count
    target = jnp.where(live, owner * limit + rank, -1)
    place = onehot(iota((npath * limit, slots), 0) == target)
    return place, inside


def start_tiles(tiles_ref, held, sems):
    step = held.shape[0] // CHUNKS
    copies = []
    for k in range(CHUNKS):
        part = pl.ds(k * step, step)
        copies.append(pltpu.make_async_copy(tiles_ref.at[part], held.at[part], sems.at[k]))
        copies[-1].start()
    return copies


def backward(held, rows, left, copies=None, turned=None):
    slots, tile = held.shape[0], held.shape[1]
    row_tiles = left.shape[0]
    row_hot = onehot(iota((row_tiles, slots), 0) == rows)
    both = split(left)
    high = dot(row_hot, both[:row_tiles], 0, 0)
    low = dot(row_hot, both[row_tiles:], 0, 0)
    step = slots // CHUNKS
    sub = iota((2 * step, tile), 0)
    out = []
    for k in range(CHUNKS):
        if copies is not None:
            copies[k].wait()
        part = slice(k * step, (k + 1) * step)
        block = jnp.concatenate([high[part], low[part]], axis=0)
        acc = jnp.zeros((2 * step, tile), F32)
        for i in range(step):
            mine = (sub == i) | (sub == i + step)
            acc += dot(jnp.where(mine, block, 0.0).astype(BF16), held[k * step + i], 1, 0)
        out.append(fold(acc).astype(BF16))
        if turned is not None and k < CHUNKS - 1:
            for i in range(TURNED):
                turned[k * TURNED + i] = held[k * step + i].T
    return jnp.concatenate(out, axis=0)


def forward(held, turned, rows, picked, row_tiles):
    slots, tile = held.shape[0], held.shape[1]
    row_hot = jnp.where(iota((row_tiles, slots), 0) == rows, 1.0, 0.0)
    acc = jnp.zeros((row_tiles, tile), F32)
    for s in range(slots):
        lhs = row_hot[:, s : s + 1] * picked[s : s + 1, :]
        k, i = divmod(s, slots // CHUNKS)
        if i < TURNED and k < CHUNKS - 1:
            acc += dot(lhs.astype(BF16), turned[k * TURNED + i], 1, 0)
        else:
            acc += dot(lhs.astype(BF16), held[s], 1, 1)
    return acc


def first_kernel(
    table_ref, tiles_ref, send_ref, held_ref, place_ref, turned_ref, sems
):
    npath, limit, width = send_ref.shape
    copies = start_tiles(tiles_ref, held_ref, sems)
    left = data_of(table_ref)
    rows, cols, count = slots_of(table_ref)
    place, inside = placement(cols, count, npath, limit)
    place_ref[...] = place
    slots = cols.shape[1]
    meta = jnp.where(iota((slots, META), 1) == 0, column_of(inside) + 1, 0)
    prods = backward(held_ref, rows, left, copies, turned_ref)
    tile = prods.shape[1]
    terms = jnp.concatenate([prods, meta.astype(F32).astype(BF16)], axis=1)
    out = dot(place, terms, 1, 0)
    lane = iota((1, META), 1)
    sent = out[:, :tile]
    extra = pieces(lane, total(left * left)) + pieces(lane - 3, total(sent * sent))
    full = jnp.concatenate([sent, out[:, tile:] + extra], axis=1)
    send_ref[...] = full.astype(BF16).reshape(npath, limit, width)


def hot_of(meta):
    return onehot(meta[:, 0:1].astype(jnp.int32) == iota((meta.shape[0], CT_DEV), 1) + 1)


def first_owner_kernel(recv_ref, send_ref, own_ref, scal_ref):
    npath, limit, width = recv_ref.shape
    tile = width - META
    recv = recv_ref[...].reshape(npath * limit, width)
    meta = recv[:, tile:].astype(F32)
    hot = hot_of(meta)
    own = dot(hot, recv[:, :tile], 0, 0)
    own_ref[...] = own
    per = jnp.sum(meta, axis=0, keepdims=True) * (1.0 / limit)
    scal_ref[...] = jnp.zeros_like(scal_ref)
    scal_ref[0:1, :] = jnp.broadcast_to(sum_pieces(per), (1, META))
    lane = iota(per.shape, 1)
    guess = jnp.sum(jnp.where((lane >= 4) & (lane <= 6), per, 0.0), axis=1, keepdims=True)
    scal_ref[1:2, :] = jnp.broadcast_to(guess, (1, META))
    send_ref[...] = dot(hot, own.astype(BF16), 1, 0).astype(BF16).reshape(npath, limit, tile)


def forward_kernel(
    table_ref, place_ref, recv_ref, tail_ref, tiles_ref, turned_ref, part_ref
):
    npath, limit, tile = recv_ref.shape
    row_tiles = part_ref.shape[0]
    rows = slots_of(table_ref)[0]
    picked = dot(place_ref[...], recv_ref[...].reshape(npath * limit, tile), 0, 0)
    part_ref[:, :tile] = forward(tiles_ref, turned_ref, rows, picked, row_tiles)
    part_ref[:, tile:] = tail_ref[...]


def second_kernel(
    table_ref, place_ref, part_ref, other_ref, scal_ref, tiles_ref,
    send_ref, image_ref, gamma_ref,
):
    npath, limit, tile = send_ref.shape
    sums = part_ref[...] + other_ref[...]
    image = sums[:, :tile]
    gamma = sums[1:2, tile : tile + 1] / (scal_ref[0:1, 0:1] + EPS)
    image_ref[...] = image
    gamma_ref[...] = jnp.broadcast_to(gamma, gamma_ref.shape)
    rows = slots_of(table_ref)[0]
    prods = backward(tiles_ref, rows, image - gamma * data_of(table_ref))
    send_ref[...] = dot(place_ref[...], prods, 1, 0).astype(BF16).reshape(npath, limit, tile)


def second_owner_kernel(recv_ref, index_ref, own_ref, send_ref, next_ref, scal_ref):
    npath, limit, tile = recv_ref.shape
    rows = npath * limit
    hot = hot_of(index_ref[:, :, tile:].reshape(rows, META).astype(F32))
    own = dot(hot, recv_ref[...].reshape(rows, tile), 0, 0)
    next_ref[...] = own
    before = own_ref[...]
    scal_ref[...] = jnp.zeros_like(scal_ref)
    for k, value in enumerate((before * before, before * own, own * own)):
        scal_ref[k : k + 1, :] = jnp.broadcast_to(total(value), (1, META))
    send_ref[...] = dot(hot, own.astype(BF16), 1, 0).astype(BF16).reshape(npath, limit, tile)


def third_kernel(table_ref, part_ref, other_ref, image_ref, send_ref, next_ref):
    npath = send_ref.shape[0]
    tile = image_ref.shape[1]
    sums = part_ref[...] + other_ref[...]
    z, x, d = sums[:, :tile], image_ref[...], data_of(table_ref)
    next_ref[...] = z
    values = [total(a * b) for a, b in ((d, d), (d, x), (x, x), (d, z), (x, z), (z, z))]
    values += [sums[k : k + 1, tile : tile + 1] for k in range(3)]
    lane = iota((1, META), 1)
    lines = [pieces(lane, v) for v in values[:8]]
    lines[0] += pieces(lane - 3, values[8])
    message = jnp.concatenate(lines, axis=0).astype(BF16)
    for q in range(npath):
        send_ref[q] = message


def final_kernel(
    total_rows, table_ref, recv_ref, next_ref, image_ref, own0_ref, own1_ref, gamma_ref,
    solution_ref, out_ref,
):
    sums = jnp.sum(recv_ref[...].astype(F32), axis=0)
    dd, dx, xx, dz, xz, zz, vv, vy = [sum_pieces(sums[k : k + 1]) for k in range(8)]
    lane = iota((1, META), 1)
    yy = total(jnp.where((lane >= 4) & (lane <= 6), sums[0:1], 0.0))
    beta0_sq = dd + EPS
    beta0 = jnp.sqrt(beta0_sq)
    alpha0_sq = vv / beta0_sq + EPS
    alpha0 = jnp.sqrt(alpha0_sq)
    scale0 = 1.0 / (beta0 * alpha0)
    beta1_sq = xx - alpha0_sq * (2.0 * dx - alpha0_sq * dd)
    beta1_sq = (jnp.sqrt(jnp.maximum(beta1_sq, 0.0)) * scale0) ** 2 + EPS
    beta1 = jnp.sqrt(beta1_sq)
    kappa = gamma_ref[0:1, 0:1] - alpha0_sq - beta1_sq
    scale1 = scale0 / beta1
    alpha1_sq = jnp.maximum(yy + kappa * (2.0 * vy + kappa * vv), 0.0)
    alpha1_sq = (jnp.sqrt(alpha1_sq) * scale1) ** 2 + EPS
    alpha1 = jnp.sqrt(alpha1_sq)
    scale2 = scale1 / alpha1
    lam, mu = kappa - alpha1_sq, alpha1_sq * alpha0_sq
    norm = zz + lam * lam * xx + mu * mu * dd + 2.0 * (lam * xz + mu * dz + lam * mu * dx)
    beta2 = jnp.sqrt((jnp.sqrt(jnp.maximum(norm, 0.0)) * scale2) ** 2 + EPS)
    rho1 = jnp.sqrt(alpha0_sq + beta1_sq)
    cosine, sine = alpha0 / rho1, beta1 / rho1
    theta = sine * alpha1
    rhobar = -cosine * alpha1
    phi1, phibar = cosine * beta0, sine * beta0
    rho2 = jnp.sqrt(rhobar * rhobar + beta2 * beta2)
    phi2 = rhobar / rho2 * phibar
    right0 = own0_ref[...] * scale0
    right1 = (own1_ref[...] + kappa * own0_ref[...]) * scale2
    search = right1 - (theta / rho1) * right0
    answer = (phi1 / rho1) * right0 + (phi2 / rho2) * search
    store_pairs(solution_ref, answer, answer.shape[0])
    left = (next_ref[...] + lam * image_ref[...] + mu * data_of(table_ref)) * scale2
    left = left * (total_rows**0.5 / beta2)
    store_pairs(out_ref, left, left.shape[0])


def call(kernel, ins, outs, scratch=(), flops=0, moved=0, room=LIMIT):
    shapes = [jax.ShapeDtypeStruct(s, d) for s, d in outs]
    return pl.pallas_call(
        kernel,
        in_specs=ins,
        out_specs=[VMEM] * len(outs),
        out_shape=shapes,
        scratch_shapes=scratch,
        compiler_params=pltpu.CompilerParams(vmem_limit_bytes=room),
        cost_estimate=pl.CostEstimate(flops=flops, bytes_accessed=moved, transcendentals=0),
    )


def on_device(tiles, tile_rows, tile_cols, tile_counts, data):
    slots, tile, _ = tiles.shape
    row_tiles = data.shape[0] // tile
    npath = lax.axis_size("path")
    limit = max(2, max(slots // 8, (slots + npath - 1) // npath))
    cells = data.shape[0] + 8 * META
    named, start = 0, data.shape[0]
    for x in (tile_cols, tile_rows, tile_counts):
        named += jnp.pad(x, (start, cells - start - x.shape[0]))
        start += x.shape[0]
    table = named.astype(F32) + jnp.pad(data, (0, cells - data.shape[0]))
    table = table.reshape(-1, META)
    payload = ((npath, limit, tile), BF16)
    scal = ((8, META), F32)
    own_shape = ((CT_DEV, tile), F32)
    left_shape = ((row_tiles, tile), F32)
    part_shape = ((row_tiles, tile + META), F32)
    work = dict(flops=2 * 8 * tiles.size, moved=2 * tiles.size)

    def swap(x):
        return lax.all_to_all(x, "path", 0, 0, tiled=True)

    def other_half(x):
        return lax.ppermute(x, "mp", [(0, 1), (1, 0)])

    send, tiles, place, turned = call(
        first_kernel,
        [VMEM, HBM],
        [
            ((npath, limit, tile + META), BF16),
            (tiles.shape, tiles.dtype),
            ((npath * limit, slots), BF16),
            (((CHUNKS - 1) * TURNED, tile, tile), tiles.dtype),
        ],
        scratch=[pltpu.SemaphoreType.DMA((CHUNKS,))],
        room=FIRST_LIMIT,
        **work,
    )(table, pltpu.with_memory_space_constraint(tiles, pltpu.HBM))
    index = swap(send)
    send, own0, scal0 = call(first_owner_kernel, [VMEM], [payload, own_shape, scal])(index)
    pass_forward = call(forward_kernel, [VMEM] * 6, [part_shape], **work)
    (part,) = pass_forward(table, place, swap(send), scal0, tiles, turned)
    send, image, gamma = call(second_kernel, [VMEM] * 6, [payload, left_shape, scal], **work)(
        table, place, part, other_half(part), scal0, tiles
    )
    send, own1, scal1 = call(second_owner_kernel, [VMEM] * 3, [payload, own_shape, scal])(
        swap(send), index, own0
    )
    (part,) = pass_forward(table, place, swap(send), scal1, tiles, turned)
    send, mixed = call(third_kernel, [VMEM] * 4, [((npath, 8, META), BF16), left_shape])(
        table, part, other_half(part), image
    )
    total_rows = row_tiles * tile * npath

    def last(*refs):
        final_kernel(total_rows, *refs)

    solution, left = call(
        last, [VMEM] * 7, [((CT_DEV * 2, tile // 2), F32), ((row_tiles * 2, tile // 2), F32)]
    )(table, swap(send), mixed, image, own0, own1, gamma)
    return solution.reshape(-1), left.reshape(-1)


def solution(mesh):
    placed = (
        P(("path", "mp"), None, None),
        P(("path", "mp")),
        P(("path", "mp")),
        P(("path", "mp")),
        P(("period", "path")),
    )
    return jax.shard_map(
        on_device,
        mesh=mesh,
        in_specs=placed,
        out_specs=(P(("period", "path", "mp")), P(("period", "path"))),
        check_vma=False,
    )
```

```python
import jax
import jax.numpy as jnp
from jax import lax
from jax.experimental import pallas as pl
from jax.experimental.pallas import tpu as pltpu
from jax.sharding import PartitionSpec as P

CT_DEV = 32
EPS = 1e-12
CHUNKS = 8
TURNED = 8
META = 128
LIMIT = 12 << 20
FIRST_LIMIT = 16 << 20
F32 = jnp.float32
BF16 = jnp.bfloat16
VMEM = pl.BlockSpec(memory_space=pltpu.VMEM)
SMEM = pl.BlockSpec(memory_space=pltpu.SMEM)
HBM = pl.BlockSpec(memory_space=pltpu.HBM)


def iota(shape, dim):
    return lax.broadcasted_iota(jnp.int32, shape, dim)


def onehot(mask):
    return jnp.where(mask, 1.0, 0.0).astype(BF16)


def dot(a, b, ca, cb):
    return lax.dot_general(a, b, (((ca,), (cb,)), ((), ())), preferred_element_type=F32)


def total(x):
    return jnp.sum(jnp.sum(x, axis=1, keepdims=True), axis=0, keepdims=True)


def load_pairs(ref, rows):
    return jnp.concatenate(
        [ref[pl.ds(0, rows, stride=2), :], ref[pl.ds(1, rows, stride=2), :]], axis=1
    )


def store_pairs(ref, value, rows):
    half = value.shape[1] // 2
    ref[pl.ds(0, rows, stride=2), :] = value[:, :half]
    ref[pl.ds(1, rows, stride=2), :] = value[:, half:]


def pieces(lane, value):
    high = value.astype(BF16).astype(F32)
    rest = value - high
    middle = rest.astype(BF16).astype(F32)
    low = rest - middle
    return jnp.where(lane == 1, high, jnp.where(lane == 2, middle, jnp.where(lane == 3, low, 0.0)))


def sum_pieces(meta):
    lane = iota(meta.shape, 1)
    return total(jnp.where((lane >= 1) & (lane <= 3), meta, 0.0))


def split(x):
    high = x.astype(BF16)
    low = (x - high.astype(F32)).astype(BF16)
    return jnp.concatenate([high, low], axis=0)


def fold(x):
    half = x.shape[0] // 2
    return x[:half] + x[half:]


def data_of(table_ref):
    return load_pairs(table_ref.at[: table_ref.shape[0] - 8], (table_ref.shape[0] - 8) // 2)


def slots_of(table_ref):
    base = table_ref.shape[0] - 8
    slots = META // 2
    both = table_ref[base : base + 1, :].astype(jnp.int32)
    count = table_ref[base + 1 : base + 2, 0:1].astype(jnp.int32)
    return both[:, slots:], both[:, :slots], count


def column_of(row):
    n = row.shape[1]
    return jnp.sum(jnp.where(iota((n, n), 0) == iota((n, n), 1), row, 0), axis=1, keepdims=True)


def placement(cols, count, npath, limit):
    slots = cols.shape[1]
    owner = lax.div(cols, CT_DEV)
    inside = cols - owner * CT_DEV
    owner_col = column_of(owner)
    earlier = iota((slots, slots), 0) < iota((slots, slots), 1)
    same = (owner_col == owner) & earlier
    rank = jnp.sum(jnp.where(same, 1, 0), axis=0, keepdims=True)
    live = iota(cols.shape, 1) < count
    target = jnp.where(live, owner * limit + rank, -1)
    place = onehot(iota((npath * limit, slots), 0) == target)
    return place, inside


def start_tiles(tiles_ref, held, sems):
    step = held.shape[0] // CHUNKS
    copies = []
    for k in range(CHUNKS):
        part = pl.ds(k * step, step)
        copies.append(pltpu.make_async_copy(tiles_ref.at[part], held.at[part], sems.at[k]))
        copies[-1].start(priority=1)
    return copies


def backward(held, rows, left, copies=None, turned=None):
    slots, tile = held.shape[0], held.shape[1]
    row_tiles = left.shape[0]
    row_hot = onehot(iota((row_tiles, slots), 0) == rows)
    both = split(left)
    high = dot(row_hot, both[:row_tiles], 0, 0)
    low = dot(row_hot, both[row_tiles:], 0, 0)
    step = slots // CHUNKS
    sub = iota((2 * step, tile), 0)
    out = []
    for k in range(CHUNKS):
        if copies is not None:
            copies[k].wait()
        part = slice(k * step, (k + 1) * step)
        block = jnp.concatenate([high[part], low[part]], axis=0)
        acc = jnp.zeros((2 * step, tile), F32)
        for i in range(step):
            mine = (sub == i) | (sub == i + step)
            acc += dot(jnp.where(mine, block, 0.0).astype(BF16), held[k * step + i], 1, 0)
        out.append(fold(acc).astype(BF16))
        if turned is not None and k < CHUNKS - 1:
            for i in range(TURNED):
                turned[k * TURNED + i] = held[k * step + i].T
    return jnp.concatenate(out, axis=0)


def forward(held, turned, rows, picked, row_tiles):
    slots, tile = held.shape[0], held.shape[1]
    row_hot = jnp.where(iota((row_tiles, slots), 0) == rows, 1.0, 0.0)
    acc = jnp.zeros((row_tiles, tile), F32)
    for s in range(slots):
        lhs = row_hot[:, s : s + 1] * picked[s : s + 1, :]
        k, i = divmod(s, slots // CHUNKS)
        if i < TURNED and k < CHUNKS - 1:
            acc += dot(lhs.astype(BF16), turned[k * TURNED + i], 1, 0)
        else:
            acc += dot(lhs.astype(BF16), held[s], 1, 1)
    return acc


def first_kernel(
    data_ref, cols_ref, rows_ref, count_ref, tiles_ref,
    send_ref, held_ref, place_ref, turned_ref, table_ref, cols_buf, rows_buf, sems, small,
):
    npath, limit, width = send_ref.shape
    lines = data_ref.shape[0]
    pairs = ((data_ref, table_ref.at[:lines]), (cols_ref, cols_buf), (rows_ref, rows_buf))
    loads = [pltpu.make_async_copy(a, b, small.at[k]) for k, (a, b) in enumerate(pairs)]
    for load in loads:
        load.start()
    copies = start_tiles(tiles_ref, held_ref, sems)
    for load in loads:
        load.wait()
    named = jnp.concatenate([cols_buf[...], rows_buf[...]], axis=1).astype(F32)
    table_ref[lines:, :] = jnp.where(iota((8, META), 0) == 0, named, 1.0 * count_ref[0])
    left = data_of(table_ref)
    rows, cols, count = slots_of(table_ref)
    place, inside = placement(cols, count, npath, limit)
    place_ref[...] = place
    slots = cols.shape[1]
    meta = jnp.where(iota((slots, META), 1) == 0, column_of(inside) + 1, 0)
    prods = backward(held_ref, rows, left, copies, turned_ref)
    tile = prods.shape[1]
    terms = jnp.concatenate([prods, meta.astype(F32).astype(BF16)], axis=1)
    out = dot(place, terms, 1, 0)
    lane = iota((1, META), 1)
    sent = out[:, :tile]
    extra = pieces(lane, total(left * left)) + pieces(lane - 3, total(sent * sent))
    full = jnp.concatenate([sent, out[:, tile:] + extra], axis=1)
    send_ref[...] = full.astype(BF16).reshape(npath, limit, width)


def hot_of(meta):
    return onehot(meta[:, 0:1].astype(jnp.int32) == iota((meta.shape[0], CT_DEV), 1) + 1)


def first_owner_kernel(recv_ref, send_ref, own_ref, scal_ref):
    npath, limit, width = recv_ref.shape
    tile = width - META
    recv = recv_ref[...].reshape(npath * limit, width)
    meta = recv[:, tile:].astype(F32)
    hot = hot_of(meta)
    own = dot(hot, recv[:, :tile], 0, 0)
    own_ref[...] = own
    per = jnp.sum(meta, axis=0, keepdims=True) * (1.0 / limit)
    scal_ref[...] = jnp.zeros_like(scal_ref)
    scal_ref[0:1, :] = jnp.broadcast_to(sum_pieces(per), (1, META))
    lane = iota(per.shape, 1)
    guess = jnp.sum(jnp.where((lane >= 4) & (lane <= 6), per, 0.0), axis=1, keepdims=True)
    scal_ref[1:2, :] = jnp.broadcast_to(guess, (1, META))
    send_ref[...] = dot(hot, own.astype(BF16), 1, 0).astype(BF16).reshape(npath, limit, tile)


def forward_kernel(
    table_ref, place_ref, recv_ref, tail_ref, tiles_ref, turned_ref, part_ref
):
    npath, limit, tile = recv_ref.shape
    row_tiles = part_ref.shape[0]
    rows = slots_of(table_ref)[0]
    picked = dot(place_ref[...], recv_ref[...].reshape(npath * limit, tile), 0, 0)
    part_ref[:, :tile] = forward(tiles_ref, turned_ref, rows, picked, row_tiles)
    part_ref[:, tile:] = tail_ref[...]


def second_kernel(
    table_ref, place_ref, part_ref, other_ref, scal_ref, tiles_ref,
    send_ref, image_ref, gamma_ref,
):
    npath, limit, tile = send_ref.shape
    sums = part_ref[...] + other_ref[...]
    image = sums[:, :tile]
    gamma = sums[1:2, tile : tile + 1] / (scal_ref[0:1, 0:1] + EPS)
    image_ref[...] = image
    gamma_ref[...] = jnp.broadcast_to(gamma, gamma_ref.shape)
    rows = slots_of(table_ref)[0]
    prods = backward(tiles_ref, rows, image - gamma * data_of(table_ref))
    send_ref[...] = dot(place_ref[...], prods, 1, 0).astype(BF16).reshape(npath, limit, tile)


def second_owner_kernel(recv_ref, index_ref, own_ref, send_ref, next_ref, scal_ref):
    npath, limit, tile = recv_ref.shape
    rows = npath * limit
    hot = hot_of(index_ref[:, :, tile:].reshape(rows, META).astype(F32))
    own = dot(hot, recv_ref[...].reshape(rows, tile), 0, 0)
    next_ref[...] = own
    before = own_ref[...]
    scal_ref[...] = jnp.zeros_like(scal_ref)
    for k, value in enumerate((before * before, before * own, own * own)):
        scal_ref[k : k + 1, :] = jnp.broadcast_to(total(value), (1, META))
    send_ref[...] = dot(hot, own.astype(BF16), 1, 0).astype(BF16).reshape(npath, limit, tile)


def third_kernel(table_ref, part_ref, other_ref, image_ref, send_ref, next_ref):
    npath = send_ref.shape[0]
    tile = image_ref.shape[1]
    sums = part_ref[...] + other_ref[...]
    z, x, d = sums[:, :tile], image_ref[...], data_of(table_ref)
    next_ref[...] = z
    values = [total(a * b) for a, b in ((d, d), (d, x), (x, x), (d, z), (x, z), (z, z))]
    values += [sums[k : k + 1, tile : tile + 1] for k in range(3)]
    lane = iota((1, META), 1)
    lines = [pieces(lane, v) for v in values[:8]]
    lines[0] += pieces(lane - 3, values[8])
    message = jnp.concatenate(lines, axis=0).astype(BF16)
    for q in range(npath):
        send_ref[q] = message


def final_kernel(
    total_rows, table_ref, recv_ref, next_ref, image_ref, own0_ref, own1_ref, gamma_ref,
    solution_ref, out_ref,
):
    sums = jnp.sum(recv_ref[...].astype(F32), axis=0)
    dd, dx, xx, dz, xz, zz, vv, vy = [sum_pieces(sums[k : k + 1]) for k in range(8)]
    lane = iota((1, META), 1)
    yy = total(jnp.where((lane >= 4) & (lane <= 6), sums[0:1], 0.0))
    beta0_sq = dd + EPS
    beta0 = jnp.sqrt(beta0_sq)
    alpha0_sq = vv / beta0_sq + EPS
    alpha0 = jnp.sqrt(alpha0_sq)
    scale0 = 1.0 / (beta0 * alpha0)
    beta1_sq = xx - alpha0_sq * (2.0 * dx - alpha0_sq * dd)
    beta1_sq = (jnp.sqrt(jnp.maximum(beta1_sq, 0.0)) * scale0) ** 2 + EPS
    beta1 = jnp.sqrt(beta1_sq)
    kappa = gamma_ref[0:1, 0:1] - alpha0_sq - beta1_sq
    scale1 = scale0 / beta1
    alpha1_sq = jnp.maximum(yy + kappa * (2.0 * vy + kappa * vv), 0.0)
    alpha1_sq = (jnp.sqrt(alpha1_sq) * scale1) ** 2 + EPS
    alpha1 = jnp.sqrt(alpha1_sq)
    scale2 = scale1 / alpha1
    lam, mu = kappa - alpha1_sq, alpha1_sq * alpha0_sq
    norm = zz + lam * lam * xx + mu * mu * dd + 2.0 * (lam * xz + mu * dz + lam * mu * dx)
    beta2 = jnp.sqrt((jnp.sqrt(jnp.maximum(norm, 0.0)) * scale2) ** 2 + EPS)
    rho1 = jnp.sqrt(alpha0_sq + beta1_sq)
    cosine, sine = alpha0 / rho1, beta1 / rho1
    theta = sine * alpha1
    rhobar = -cosine * alpha1
    phi1, phibar = cosine * beta0, sine * beta0
    rho2 = jnp.sqrt(rhobar * rhobar + beta2 * beta2)
    phi2 = rhobar / rho2 * phibar
    right0 = own0_ref[...] * scale0
    right1 = (own1_ref[...] + kappa * own0_ref[...]) * scale2
    search = right1 - (theta / rho1) * right0
    answer = (phi1 / rho1) * right0 + (phi2 / rho2) * search
    store_pairs(solution_ref, answer, answer.shape[0])
    left = (next_ref[...] + lam * image_ref[...] + mu * data_of(table_ref)) * scale2
    left = left * (total_rows**0.5 / beta2)
    store_pairs(out_ref, left, left.shape[0])


def call(kernel, ins, outs, scratch=(), flops=0, moved=0, room=LIMIT):
    shapes = [jax.ShapeDtypeStruct(s, d) for s, d in outs]
    return pl.pallas_call(
        kernel,
        in_specs=ins,
        out_specs=[VMEM] * len(outs),
        out_shape=shapes,
        scratch_shapes=scratch,
        compiler_params=pltpu.CompilerParams(vmem_limit_bytes=room),
        cost_estimate=pl.CostEstimate(flops=flops, bytes_accessed=moved, transcendentals=0),
    )


def on_device(tiles, tile_rows, tile_cols, tile_counts, data):
    slots, tile, _ = tiles.shape
    row_tiles = data.shape[0] // tile
    npath = lax.axis_size("path")
    limit = max(2, max(slots // 8, (slots + npath - 1) // npath))
    data = data.reshape(-1, META)
    payload = ((npath, limit, tile), BF16)
    scal = ((8, META), F32)
    own_shape = ((CT_DEV, tile), F32)
    left_shape = ((row_tiles, tile), F32)
    part_shape = ((row_tiles, tile + META), F32)
    work = dict(flops=2 * 8 * tiles.size, moved=2 * tiles.size)

    def swap(x):
        return lax.all_to_all(x, "path", 0, 0, tiled=True)

    def other_half(x):
        return lax.ppermute(x, "mp", [(0, 1), (1, 0)])

    inputs = [data, tile_cols.reshape(1, slots), tile_rows.reshape(1, slots), tiles]
    inputs = [pltpu.with_memory_space_constraint(x, pltpu.HBM) for x in inputs]
    send, tiles, place, turned, table = call(
        first_kernel,
        [HBM] * 3 + [SMEM, HBM],
        [
            ((npath, limit, tile + META), BF16),
            (tiles.shape, tiles.dtype),
            ((npath * limit, slots), BF16),
            (((CHUNKS - 1) * TURNED, tile, tile), tiles.dtype),
            ((data.shape[0] + 8, META), F32),
        ],
        scratch=[
            pltpu.VMEM((1, slots), jnp.int32),
            pltpu.VMEM((1, slots), jnp.int32),
            pltpu.SemaphoreType.DMA((CHUNKS,)),
            pltpu.SemaphoreType.DMA((3,)),
        ],
        room=FIRST_LIMIT,
        **work,
    )(*inputs[:3], tile_counts, inputs[3])
    index = swap(send)
    send, own0, scal0 = call(first_owner_kernel, [VMEM], [payload, own_shape, scal])(index)
    pass_forward = call(forward_kernel, [VMEM] * 6, [part_shape], **work)
    (part,) = pass_forward(table, place, swap(send), scal0, tiles, turned)
    send, image, gamma = call(second_kernel, [VMEM] * 6, [payload, left_shape, scal], **work)(
        table, place, part, other_half(part), scal0, tiles
    )
    send, own1, scal1 = call(second_owner_kernel, [VMEM] * 3, [payload, own_shape, scal])(
        swap(send), index, own0
    )
    (part,) = pass_forward(table, place, swap(send), scal1, tiles, turned)
    send, mixed = call(third_kernel, [VMEM] * 4, [((npath, 8, META), BF16), left_shape])(
        table, part, other_half(part), image
    )
    total_rows = row_tiles * tile * npath

    def last(*refs):
        final_kernel(total_rows, *refs)

    solution, left = call(
        last, [VMEM] * 7, [((CT_DEV * 2, tile // 2), F32), ((row_tiles * 2, tile // 2), F32)]
    )(table, swap(send), mixed, image, own0, own1, gamma)
    return solution.reshape(-1), left.reshape(-1)


def solution(mesh):
    placed = (
        P(("path", "mp"), None, None),
        P(("path", "mp")),
        P(("path", "mp")),
        P(("path", "mp")),
        P(("period", "path")),
    )
    return jax.shard_map(
        on_device,
        mesh=mesh,
        in_specs=placed,
        out_specs=(P(("period", "path", "mp")), P(("period", "path"))),
        check_vma=False,
    )
```

```python
import jax
import jax.numpy as jnp
from jax import lax
from jax.experimental import pallas as pl
from jax.experimental.pallas import tpu as pltpu
from jax.sharding import PartitionSpec as P

CT_DEV = 32
EPS = 1e-12
CHUNKS = 8
TURNED = 8
META = 128
LIMIT = 12 << 20
FIRST_LIMIT = 16 << 20
F32 = jnp.float32
BF16 = jnp.bfloat16
VMEM = pl.BlockSpec(memory_space=pltpu.VMEM)
SMEM = pl.BlockSpec(memory_space=pltpu.SMEM)
HBM = pl.BlockSpec(memory_space=pltpu.HBM)


def iota(shape, dim):
    return lax.broadcasted_iota(jnp.int32, shape, dim)


def onehot(mask):
    return jnp.where(mask, 1.0, 0.0).astype(BF16)


def dot(a, b, ca, cb):
    return lax.dot_general(a, b, (((ca,), (cb,)), ((), ())), preferred_element_type=F32)


def total(x):
    return jnp.sum(jnp.sum(x, axis=1, keepdims=True), axis=0, keepdims=True)


def load_pairs(ref, rows):
    return jnp.concatenate(
        [ref[pl.ds(0, rows, stride=2), :], ref[pl.ds(1, rows, stride=2), :]], axis=1
    )


def store_pairs(ref, value, rows):
    half = value.shape[1] // 2
    ref[pl.ds(0, rows, stride=2), :] = value[:, :half]
    ref[pl.ds(1, rows, stride=2), :] = value[:, half:]


def pieces(lane, value):
    high = value.astype(BF16).astype(F32)
    rest = value - high
    middle = rest.astype(BF16).astype(F32)
    low = rest - middle
    return jnp.where(lane == 1, high, jnp.where(lane == 2, middle, jnp.where(lane == 3, low, 0.0)))


def sum_pieces(meta):
    lane = iota(meta.shape, 1)
    return total(jnp.where((lane >= 1) & (lane <= 3), meta, 0.0))


def split(x):
    high = x.astype(BF16)
    low = (x - high.astype(F32)).astype(BF16)
    return jnp.concatenate([high, low], axis=0)


def fold(x):
    half = x.shape[0] // 2
    return x[:half] + x[half:]


def data_of(table_ref):
    return load_pairs(table_ref.at[: table_ref.shape[0] - 8], (table_ref.shape[0] - 8) // 2)


def slots_of(table_ref):
    base = table_ref.shape[0] - 8
    slots = META // 2
    both = table_ref[base : base + 1, :].astype(jnp.int32)
    count = table_ref[base + 1 : base + 2, 0:1].astype(jnp.int32)
    return both[:, slots:], both[:, :slots], count


def column_of(row):
    n = row.shape[1]
    return jnp.sum(jnp.where(iota((n, n), 0) == iota((n, n), 1), row, 0), axis=1, keepdims=True)


def placement(cols, count, npath, limit):
    slots = cols.shape[1]
    owner = lax.div(cols, CT_DEV)
    inside = cols - owner * CT_DEV
    owner_col = column_of(owner)
    earlier = iota((slots, slots), 0) < iota((slots, slots), 1)
    same = (owner_col == owner) & earlier
    rank = jnp.sum(jnp.where(same, 1, 0), axis=0, keepdims=True)
    live = iota(cols.shape, 1) < count
    target = jnp.where(live, owner * limit + rank, -1)
    place = onehot(iota((npath * limit, slots), 0) == target)
    return place, inside


def start_tiles(tiles_ref, held, sems):
    step = held.shape[0] // CHUNKS
    copies = []
    for k in range(CHUNKS):
        part = pl.ds(k * step, step)
        copies.append(pltpu.make_async_copy(tiles_ref.at[part], held.at[part], sems.at[k]))
        copies[-1].start(priority=1)
    return copies


def backward(held, rows, left, copies=None, turned=None):
    slots, tile = held.shape[0], held.shape[1]
    row_tiles = left.shape[0]
    row_hot = onehot(iota((row_tiles, slots), 0) == rows)
    both = split(left)
    high = dot(row_hot, both[:row_tiles], 0, 0)
    low = dot(row_hot, both[row_tiles:], 0, 0)
    step = slots // CHUNKS
    sub = iota((2 * step, tile), 0)
    out = []
    for k in range(CHUNKS):
        if copies is not None:
            copies[k].wait()
        part = slice(k * step, (k + 1) * step)
        block = jnp.concatenate([high[part], low[part]], axis=0)
        acc = jnp.zeros((2 * step, tile), F32)
        for i in range(step):
            mine = (sub == i) | (sub == i + step)
            acc += dot(jnp.where(mine, block, 0.0).astype(BF16), held[k * step + i], 1, 0)
        out.append(fold(acc).astype(BF16))
        if turned is not None:
            for i in range(TURNED):
                turned[k * TURNED + i] = held[k * step + i].T
    return jnp.concatenate(out, axis=0)


def forward(held, turned, rows, picked, row_tiles):
    slots, tile = held.shape[0], held.shape[1]
    row_hot = jnp.where(iota((row_tiles, slots), 0) == rows, 1.0, 0.0)
    acc = jnp.zeros((row_tiles, tile), F32)
    for s in range(slots):
        lhs = row_hot[:, s : s + 1] * picked[s : s + 1, :]
        k, i = divmod(s, slots // CHUNKS)
        if i < TURNED:
            acc += dot(lhs.astype(BF16), turned[k * TURNED + i], 1, 0)
        else:
            acc += dot(lhs.astype(BF16), held[s], 1, 1)
    return acc


def first_kernel(
    data_ref, cols_ref, rows_ref, count_ref, tiles_ref,
    send_ref, held_ref, place_ref, turned_ref, table_ref, cols_buf, rows_buf, sems, small,
):
    npath, limit, width = send_ref.shape
    lines = data_ref.shape[0]
    pairs = ((data_ref, table_ref.at[:lines]), (cols_ref, cols_buf), (rows_ref, rows_buf))
    loads = [pltpu.make_async_copy(a, b, small.at[k]) for k, (a, b) in enumerate(pairs)]
    for load in loads:
        load.start()
    copies = start_tiles(tiles_ref, held_ref, sems)
    for load in loads:
        load.wait()
    named = jnp.concatenate([cols_buf[...], rows_buf[...]], axis=1).astype(F32)
    table_ref[lines:, :] = jnp.where(iota((8, META), 0) == 0, named, 1.0 * count_ref[0])
    left = data_of(table_ref)
    rows, cols, count = slots_of(table_ref)
    place, inside = placement(cols, count, npath, limit)
    place_ref[...] = place
    slots = cols.shape[1]
    meta = jnp.where(iota((slots, META), 1) == 0, column_of(inside) + 1, 0)
    prods = backward(held_ref, rows, left, copies, turned_ref)
    tile = prods.shape[1]
    terms = jnp.concatenate([prods, meta.astype(F32).astype(BF16)], axis=1)
    out = dot(place, terms, 1, 0)
    lane = iota((1, META), 1)
    sent = out[:, :tile]
    extra = pieces(lane, total(left * left)) + pieces(lane - 3, total(sent * sent))
    full = jnp.concatenate([sent, out[:, tile:] + extra], axis=1)
    send_ref[...] = full.astype(BF16).reshape(npath, limit, width)


def hot_of(meta):
    return onehot(meta[:, 0:1].astype(jnp.int32) == iota((meta.shape[0], CT_DEV), 1) + 1)


def first_owner_kernel(recv_ref, send_ref, own_ref, scal_ref):
    npath, limit, width = recv_ref.shape
    tile = width - META
    recv = recv_ref[...].reshape(npath * limit, width)
    meta = recv[:, tile:].astype(F32)
    hot = hot_of(meta)
    own = dot(hot, recv[:, :tile], 0, 0)
    own_ref[...] = own
    per = jnp.sum(meta, axis=0, keepdims=True) * (1.0 / limit)
    scal_ref[...] = jnp.zeros_like(scal_ref)
    scal_ref[0:1, :] = jnp.broadcast_to(sum_pieces(per), (1, META))
    lane = iota(per.shape, 1)
    guess = jnp.sum(jnp.where((lane >= 4) & (lane <= 6), per, 0.0), axis=1, keepdims=True)
    scal_ref[1:2, :] = jnp.broadcast_to(guess, (1, META))
    send_ref[...] = dot(hot, own.astype(BF16), 1, 0).astype(BF16).reshape(npath, limit, tile)


def forward_kernel(
    table_ref, place_ref, recv_ref, tail_ref, tiles_ref, turned_ref, part_ref
):
    npath, limit, tile = recv_ref.shape
    row_tiles = part_ref.shape[0]
    rows = slots_of(table_ref)[0]
    picked = dot(place_ref[...], recv_ref[...].reshape(npath * limit, tile), 0, 0)
    part_ref[:, :tile] = forward(tiles_ref, turned_ref, rows, picked, row_tiles)
    part_ref[:, tile:] = tail_ref[...]


def second_kernel(
    table_ref, place_ref, part_ref, other_ref, scal_ref, tiles_ref,
    send_ref, image_ref, gamma_ref,
):
    npath, limit, tile = send_ref.shape
    sums = part_ref[...] + other_ref[...]
    image = sums[:, :tile]
    gamma = sums[1:2, tile : tile + 1] / (scal_ref[0:1, 0:1] + EPS)
    image_ref[...] = image
    gamma_ref[...] = jnp.broadcast_to(gamma, gamma_ref.shape)
    rows = slots_of(table_ref)[0]
    prods = backward(tiles_ref, rows, image - gamma * data_of(table_ref))
    send_ref[...] = dot(place_ref[...], prods, 1, 0).astype(BF16).reshape(npath, limit, tile)


def second_owner_kernel(recv_ref, index_ref, own_ref, send_ref, next_ref, scal_ref):
    npath, limit, tile = recv_ref.shape
    rows = npath * limit
    hot = hot_of(index_ref[:, :, tile:].reshape(rows, META).astype(F32))
    own = dot(hot, recv_ref[...].reshape(rows, tile), 0, 0)
    next_ref[...] = own
    before = own_ref[...]
    scal_ref[...] = jnp.zeros_like(scal_ref)
    for k, value in enumerate((before * before, before * own, own * own)):
        scal_ref[k : k + 1, :] = jnp.broadcast_to(total(value), (1, META))
    send_ref[...] = dot(hot, own.astype(BF16), 1, 0).astype(BF16).reshape(npath, limit, tile)


def third_kernel(table_ref, part_ref, other_ref, image_ref, send_ref, next_ref):
    npath = send_ref.shape[0]
    tile = image_ref.shape[1]
    sums = part_ref[...] + other_ref[...]
    z, x, d = sums[:, :tile], image_ref[...], data_of(table_ref)
    next_ref[...] = z
    values = [total(a * b) for a, b in ((d, d), (d, x), (x, x), (d, z), (x, z), (z, z))]
    values += [sums[k : k + 1, tile : tile + 1] for k in range(3)]
    lane = iota((1, META), 1)
    lines = [pieces(lane, v) for v in values[:8]]
    lines[0] += pieces(lane - 3, values[8])
    message = jnp.concatenate(lines, axis=0).astype(BF16)
    for q in range(npath):
        send_ref[q] = message


def final_kernel(
    total_rows, table_ref, recv_ref, next_ref, image_ref, own0_ref, own1_ref, gamma_ref,
    solution_ref, out_ref,
):
    sums = jnp.sum(recv_ref[...].astype(F32), axis=0)
    dd, dx, xx, dz, xz, zz, vv, vy = [sum_pieces(sums[k : k + 1]) for k in range(8)]
    lane = iota((1, META), 1)
    yy = total(jnp.where((lane >= 4) & (lane <= 6), sums[0:1], 0.0))
    beta0_sq = dd + EPS
    beta0 = jnp.sqrt(beta0_sq)
    alpha0_sq = vv / beta0_sq + EPS
    alpha0 = jnp.sqrt(alpha0_sq)
    scale0 = 1.0 / (beta0 * alpha0)
    beta1_sq = xx - alpha0_sq * (2.0 * dx - alpha0_sq * dd)
    beta1_sq = (jnp.sqrt(jnp.maximum(beta1_sq, 0.0)) * scale0) ** 2 + EPS
    beta1 = jnp.sqrt(beta1_sq)
    kappa = gamma_ref[0:1, 0:1] - alpha0_sq - beta1_sq
    scale1 = scale0 / beta1
    alpha1_sq = jnp.maximum(yy + kappa * (2.0 * vy + kappa * vv), 0.0)
    alpha1_sq = (jnp.sqrt(alpha1_sq) * scale1) ** 2 + EPS
    alpha1 = jnp.sqrt(alpha1_sq)
    scale2 = scale1 / alpha1
    lam, mu = kappa - alpha1_sq, alpha1_sq * alpha0_sq
    norm = zz + lam * lam * xx + mu * mu * dd + 2.0 * (lam * xz + mu * dz + lam * mu * dx)
    beta2 = jnp.sqrt((jnp.sqrt(jnp.maximum(norm, 0.0)) * scale2) ** 2 + EPS)
    rho1 = jnp.sqrt(alpha0_sq + beta1_sq)
    cosine, sine = alpha0 / rho1, beta1 / rho1
    theta = sine * alpha1
    rhobar = -cosine * alpha1
    phi1, phibar = cosine * beta0, sine * beta0
    rho2 = jnp.sqrt(rhobar * rhobar + beta2 * beta2)
    phi2 = rhobar / rho2 * phibar
    right0 = own0_ref[...] * scale0
    right1 = (own1_ref[...] + kappa * own0_ref[...]) * scale2
    search = right1 - (theta / rho1) * right0
    answer = (phi1 / rho1) * right0 + (phi2 / rho2) * search
    store_pairs(solution_ref, answer, answer.shape[0])
    left = (next_ref[...] + lam * image_ref[...] + mu * data_of(table_ref)) * scale2
    left = left * (total_rows**0.5 / beta2)
    store_pairs(out_ref, left, left.shape[0])


def call(kernel, ins, outs, scratch=(), flops=0, moved=0, room=LIMIT):
    shapes = [jax.ShapeDtypeStruct(s, d) for s, d in outs]
    return pl.pallas_call(
        kernel,
        in_specs=ins,
        out_specs=[VMEM] * len(outs),
        out_shape=shapes,
        scratch_shapes=scratch,
        compiler_params=pltpu.CompilerParams(vmem_limit_bytes=room),
        cost_estimate=pl.CostEstimate(flops=flops, bytes_accessed=moved, transcendentals=0),
    )


def on_device(tiles, tile_rows, tile_cols, tile_counts, data):
    slots, tile, _ = tiles.shape
    row_tiles = data.shape[0] // tile
    npath = lax.axis_size("path")
    limit = max(2, max(slots // 8, (slots + npath - 1) // npath))
    data = data.reshape(-1, META)
    payload = ((npath, limit, tile), BF16)
    scal = ((8, META), F32)
    own_shape = ((CT_DEV, tile), F32)
    left_shape = ((row_tiles, tile), F32)
    part_shape = ((row_tiles, tile + META), F32)
    work = dict(flops=2 * 8 * tiles.size, moved=2 * tiles.size)

    def swap(x):
        return lax.all_to_all(x, "path", 0, 0, tiled=True)

    def other_half(x):
        return lax.ppermute(x, "mp", [(0, 1), (1, 0)])

    inputs = [data, tile_cols.reshape(1, slots), tile_rows.reshape(1, slots), tiles]
    inputs = [pltpu.with_memory_space_constraint(x, pltpu.HBM) for x in inputs]
    send, tiles, place, turned, table = call(
        first_kernel,
        [HBM] * 3 + [SMEM, HBM],
        [
            ((npath, limit, tile + META), BF16),
            (tiles.shape, tiles.dtype),
            ((npath * limit, slots), BF16),
            ((CHUNKS * TURNED, tile, tile), tiles.dtype),
            ((data.shape[0] + 8, META), F32),
        ],
        scratch=[
            pltpu.VMEM((1, slots), jnp.int32),
            pltpu.VMEM((1, slots), jnp.int32),
            pltpu.SemaphoreType.DMA((CHUNKS,)),
            pltpu.SemaphoreType.DMA((3,)),
        ],
        room=FIRST_LIMIT,
        **work,
    )(*inputs[:3], tile_counts, inputs[3])
    index = swap(send)
    send, own0, scal0 = call(first_owner_kernel, [VMEM], [payload, own_shape, scal])(index)
    pass_forward = call(forward_kernel, [VMEM] * 6, [part_shape], **work)
    (part,) = pass_forward(table, place, swap(send), scal0, tiles, turned)
    send, image, gamma = call(second_kernel, [VMEM] * 6, [payload, left_shape, scal], **work)(
        table, place, part, other_half(part), scal0, tiles
    )
    send, own1, scal1 = call(second_owner_kernel, [VMEM] * 3, [payload, own_shape, scal])(
        swap(send), index, own0
    )
    (part,) = pass_forward(table, place, swap(send), scal1, tiles, turned)
    send, mixed = call(third_kernel, [VMEM] * 4, [((npath, 8, META), BF16), left_shape])(
        table, part, other_half(part), image
    )
    total_rows = row_tiles * tile * npath

    def last(*refs):
        final_kernel(total_rows, *refs)

    solution, left = call(
        last, [VMEM] * 7, [((CT_DEV * 2, tile // 2), F32), ((row_tiles * 2, tile // 2), F32)]
    )(table, swap(send), mixed, image, own0, own1, gamma)
    return solution.reshape(-1), left.reshape(-1)


def solution(mesh):
    placed = (
        P(("path", "mp"), None, None),
        P(("path", "mp")),
        P(("path", "mp")),
        P(("path", "mp")),
        P(("period", "path")),
    )
    return jax.shard_map(
        on_device,
        mesh=mesh,
        in_specs=placed,
        out_specs=(P(("period", "path", "mp")), P(("period", "path"))),
        check_vma=False,
    )
```
